128 devices in a mesh: dp: 4 (over z), expert: 32 (over y, x, core).
Axes of the slice: x: 4, y: 4, z: 4, core: 2. Of those that a mesh axis runs over, the one named last changes fastest.
Arguments:
- tokens: bfloat16 [16384, 2048], P(('dp', 'expert')), may hold values from -6 to 6
- out_grad: bfloat16 [16384, 2048], P(('dp', 'expert')), may hold values from -6 to 6
- gate_saved: bfloat16 [16384, 6, 1408], P(('dp', 'expert')), may hold values from -6 to 6
- probs: float32 [16384, 6], P(('dp', 'expert')), may hold values from 0.1 to 1
- expert_ids: int32 [16384, 6], P(('dp', 'expert')), may hold values from 0 to 31, all different within a row; in each aligned block of 128 rows (0 to 127, 128 to 255, ...) at most 48 rows name the same one
- w_gate: bfloat16 [32, 2048, 1408], P('expert'), may hold values from -0.125 to 0.125
- w_up: bfloat16 [32, 2048, 1408], P('expert'), may hold values from -0.125 to 0.125
- w_down: bfloat16 [32, 1408, 2048], P('expert'), may hold values from -0.15625 to 0.15625
Outputs:
- input_grad: bfloat16 [16384, 2048], P(('dp', 'expert'))
- grad_gate: bfloat16 [32, 2048, 1408], P('expert', 'dp')
- grad_up: bfloat16 [32, 2048, 1408], P('expert', 'dp')
- grad_down: bfloat16 [32, 1408, 2048], P('expert', 'dp')
The draws below stay inside these ranges and needn't reach their ends.
Inputs may be any that keep to these rules, and one draw needn't show every extreme that they name: `expert_ids`: each token names 6 different experts. Among the 128 tokens of one aligned block (the tokens of one device) no expert is named more than 48 times, and in some block some expert is named exactly 48 times.
All inputs are finite; a program needn't handle non-finite values.
Results may differ from the reference program's by a relative error of at most 0.013.
Values may be sent and summed in bfloat16 or wider, within the bound.
A program may use at most 192 MiB of HBM per device.

```python
import math
import jax
import jax.numpy as jnp
import numpy as np
from jax import lax

D = 2048
H = 1408
TOP = 6
TOK_DEV = 128
EXPERTS = 32
MOST = 48
TOKENS = 16384
N_DP = 4
N_EXPERT = 32


def steps_of(stream_key, dims, shards, smallest, largest):
    gain = 1.0
    for dim, blocks in shards:
        draws = jax.random.uniform(jax.random.fold_in(jax.random.fold_in(stream_key, 6), dim), (blocks,), jnp.float32, smallest / len(shards), largest / len(shards))
        gain = gain * jnp.repeat(jnp.exp(draws), dims[dim] // blocks).reshape((-1,) + (1,) * (len(dims) - 1 - dim))
    return gain


def assign_block(key, own, number, rows, number_of, top, reach, slope):
    ranking = jax.random.permutation(key, number_of)
    crowded, common = portions_of(number_of, rows * top, reach, slope, True), portions_of(number_of, rows * top, reach, slope, False)
    places = jnp.arange(number_of)

    def named(lengths, rotation):
        used = int((lengths > 0).sum())
        fixed = max(1, used // 4)
        moved = fixed + (places - fixed + rotation * (used - fixed)) % max(1, number_of - fixed)
        return jnp.zeros((number_of,), jnp.int32).at[ranking[jnp.where(places < fixed, places, moved)]].set(jnp.asarray(lengths, jnp.int32))

    lengths = jnp.where(number % 4 == 0, named(crowded, number // 4), named(common, number - number // 4 - 1))
    mixed = jax.random.permutation(jax.random.fold_in(own, 3), number_of)
    source_of, receiver = mixed[0:number_of // 2 * 2:2], mixed[1:number_of // 2 * 2:2]
    slack = jnp.minimum(lengths[source_of] - 1, reach - lengths[receiver]) // 2
    slack = jnp.where((source_of == ranking[0]) | (receiver == ranking[0]) | (lengths[receiver] == 0), 0, jnp.maximum(slack, 0))
    moved = jax.random.randint(jax.random.fold_in(own, 4), (number_of // 2,), 0, 1 << 20) % (slack + 1)
    lengths = lengths.at[source_of].add(-moved).at[receiver].add(moved)
    labels = jnp.searchsorted(jnp.cumsum(lengths), jnp.arange(rows * top), side="right").astype(jnp.int32)
    listing = labels.reshape(top, rows).T
    listing = listing[jax.random.permutation(jax.random.fold_in(own, 1), rows)]
    rotation = jax.random.randint(jax.random.fold_in(own, 2), (rows, 1), 0, top)
    return jnp.take_along_axis(listing, (jnp.arange(top)[None, :] + rotation) % top, axis=1)


def portions_of(number_of, total, limit, skew, full):
    loads = [(1 << 20) // math.isqrt(rank ** skew) + 1 for rank in range(1, number_of + 1)]
    largest = limit if full else min(limit, max(-(-total // number_of), total * loads[0] // sum(loads)))
    least = 1 if total - largest >= number_of - 1 else 0
    holding, spare = [largest] + [least] * (number_of - 1), total - largest - least * (number_of - 1)
    while spare > 0:
        movable = [i for i in range(1, number_of) if holding[i] < largest] or [i for i in range(1, number_of) if holding[i] < limit]
        whole, left = sum([loads[i] for i in movable]), spare
        for i in movable:
            extra = min(limit - holding[i], max(1, left * loads[i] // whole), spare)
            holding[i] = holding[i] + extra
            spare = spare - extra
    return np.array(holding)


def normal_values(own_key, dims, spread, limit, pieces=(), kind=jnp.bfloat16):
    drawn = spread * jax.random.normal(own_key, dims, jnp.float32)
    if pieces:
        drawn = drawn * steps_of(own_key, dims, pieces, -0.22, 0.18)
    return jnp.clip(drawn, -limit, limit).astype(kind)


def setup_inputs(seed: int = 0) -> dict:
    key_list = jax.random.split(jax.random.key(seed), 9)
    tokens = normal_values(key_list[0], (TOKENS, D), 1.0, 6.0, ((0, 128),))
    out_grad = normal_values(key_list[1], (TOKENS, D), 1.0, 6.0, ((0, 128),))
    gate_saved = normal_values(key_list[2], (TOKENS, TOP, H), 1.5, 6.0, ((0, 128),))
    probs = jnp.clip(jnp.exp(math.log(1.0) - 2.3025851 * jax.random.uniform(key_list[3], (TOKENS, TOP), jnp.float32) ** steps_of(key_list[3], (TOKENS, TOP), ((0, 128),), -0.2, 0.2)), 0.1, 1.0)
    expert_ids_keys = jax.random.split(jax.random.fold_in(key_list[4], 1), TOKENS // TOK_DEV)
    expert_ids_turns = jax.random.permutation(jax.random.fold_in(key_list[4], 3), TOKENS // TOK_DEV)
    expert_ids = jax.vmap(lambda own, number: assign_block(jax.random.fold_in(key_list[4], 2), own, number, TOK_DEV, EXPERTS, TOP, MOST, 3))(expert_ids_keys, expert_ids_turns).reshape((TOKENS, TOP))
    w_gate = normal_values(key_list[5], (EXPERTS, D, H), D ** -0.5, 0.125, ((0, 32),))
    w_up = normal_values(key_list[6], (EXPERTS, D, H), D ** -0.5, 0.125, ((0, 32),))
    w_down = normal_values(key_list[7], (EXPERTS, H, D), H ** -0.5, 0.15625, ((0, 32),))
    return {"tokens": tokens, "out_grad": out_grad, "gate_saved": gate_saved, "probs": probs, "expert_ids": expert_ids, "w_gate": w_gate, "w_up": w_up, "w_down": w_down}


grad_scale = 0.0625


def expert_rows(rows_in, routed_rows, gate_rows, gate_mat, up_mat, down_mat):
    up_act = jnp.dot(rows_in, up_mat, preferred_element_type=jnp.float32)
    gate_val = gate_rows.astype(jnp.float32)
    gate_sig = jax.nn.sigmoid(gate_val)
    gate_act = gate_val * gate_sig
    hidden_act = (gate_act * up_act).astype(jnp.bfloat16)
    hidden_grad = jnp.dot(routed_rows, down_mat.T, preferred_element_type=jnp.float32)
    up_grad = (hidden_grad * gate_act).astype(jnp.bfloat16)
    gate_grad = (hidden_grad * up_act * gate_sig * (1.0 + gate_val * (1.0 - gate_sig))).astype(jnp.bfloat16)
    input_part = (jnp.dot(gate_grad, gate_mat.T, preferred_element_type=jnp.float32)
                  + jnp.dot(up_grad, up_mat.T, preferred_element_type=jnp.float32)).astype(jnp.bfloat16)
    both_grads = jnp.concatenate([gate_grad, up_grad], axis=1)
    term_gate_up = jnp.dot(rows_in.T, both_grads, preferred_element_type=jnp.float32)
    term_down = jnp.dot(hidden_act.T, routed_rows, preferred_element_type=jnp.float32)
    return input_part, term_gate_up, term_down


def reference(tokens, out_grad, gate_saved, probs, expert_ids, w_gate, w_up, w_down):
    group_size = N_EXPERT * TOK_DEV
    slot_total = N_EXPERT * MOST
    group_routes = group_size * TOP
    routed = (probs[:, :, None] * out_grad[:, None, :].astype(jnp.float32)).astype(jnp.bfloat16)

    def per_expert(totals, expert):
        gate_mat = w_gate[expert]
        up_mat = w_up[expert]
        down_mat = w_down[expert]
        sum_gate_up = jnp.zeros((D, 2 * H), jnp.float32)
        sum_down = jnp.zeros((H, D), jnp.float32)
        for group_index in range(N_DP):
            group_start = group_index * group_size
            group_ids = expert_ids[group_start:group_start + group_size].reshape(group_routes)
            not_mine = (group_ids != expert).astype(jnp.int32)
            route_order = jnp.argsort(not_mine, stable=True)[:slot_total].astype(jnp.int32)
            matched = not_mine[route_order] == 0
            token_row = (route_order // TOP).astype(jnp.int32)
            rows_in = jnp.where(matched[:, None], tokens[group_start:group_start + group_size][token_row], 0)
            routed_rows = jnp.where(matched[:, None], routed[group_start:group_start + group_size].reshape(group_routes, D)[route_order], 0)
            gate_rows = jnp.where(matched[:, None], gate_saved[group_start:group_start + group_size].reshape(group_routes, H)[route_order], 0)
            input_part, term_gate_up, term_down = expert_rows(rows_in, routed_rows, gate_rows, gate_mat, up_mat, down_mat)
            totals = totals.at[group_start + token_row].add(jnp.where(matched[:, None], input_part.astype(jnp.float32), 0.0))
            sum_gate_up = sum_gate_up + lax.optimization_barrier(term_gate_up.astype(jnp.bfloat16)).astype(jnp.float32)
            sum_down = sum_down + lax.optimization_barrier(term_down.astype(jnp.bfloat16)).astype(jnp.float32)
        grad_gate = (grad_scale * sum_gate_up[:, :H]).astype(jnp.bfloat16)
        grad_up = (grad_scale * sum_gate_up[:, H:]).astype(jnp.bfloat16)
        grad_down = (grad_scale * sum_down).astype(jnp.bfloat16)
        return totals, (grad_gate, grad_up, grad_down)

    totals, grads = lax.scan(per_expert, jnp.zeros((TOKENS, D), jnp.float32), jnp.arange(EXPERTS, dtype=jnp.int32))
    return totals.astype(jnp.bfloat16), grads[0], grads[1], grads[2]
```

```python
import jax
import jax.numpy as jnp
from jax import lax
from jax.sharding import PartitionSpec as P

grad_scale = 0.0625
slot_cap = 48
gate_cuts = (0, 384, 896, 1408)


def mm(a, b, ca, cb):
    return lax.dot_general(a, b, (((ca,), (cb,)), ((), ())), preferred_element_type=jnp.float32)


def slot_onehot(chosen):
    n_tok = chosen.shape[1]
    before = (
        lax.broadcasted_iota(jnp.int32, (n_tok, n_tok), 0)
        < lax.broadcasted_iota(jnp.int32, (n_tok, n_tok), 1)
    ).astype(jnp.bfloat16)
    rank = mm(chosen.astype(jnp.bfloat16), before, 1, 0).astype(jnp.int32)
    slots = lax.broadcasted_iota(jnp.int32, (1, slot_cap, 1), 1)
    return (rank[:, None, :] == slots) & chosen[:, None, :]


def local(tokens, out_grad, gate_saved, probs, expert_ids, w_gate, w_up, w_down):
    n_peers = lax.axis_size("expert")
    me = lax.axis_index("expert")
    tok_rows, model_width = tokens.shape
    top_k = expert_ids.shape[1]
    hidden_width = w_up.shape[2]
    n_slots = n_peers * slot_cap
    gate_mat, up_mat, down_mat = w_gate[0], w_up[0], w_down[0]

    meta = jnp.concatenate([expert_ids.T.astype(jnp.float32), probs.T], axis=0)
    meta_all = lax.all_gather(meta, "expert", axis=0, tiled=False)
    rows_all = lax.all_gather(tokens, "expert", axis=0, tiled=True)
    grad_all = lax.all_gather(out_grad, "expert", axis=0, tiled=True)

    ids_t = expert_ids.T
    experts = lax.broadcasted_iota(jnp.int32, (n_peers, 1, 1), 0)
    named = ids_t[None] == experts
    send_hot = slot_onehot(jnp.any(named, axis=1))
    toks = lax.broadcasted_iota(jnp.int32, (1, top_k, tok_rows), 2)
    ks = lax.broadcasted_iota(jnp.int32, (1, top_k, tok_rows), 1)
    route_of = jnp.sum(jnp.where(named, toks * top_k + ks, 0), axis=1)
    route_of_slot = jnp.sum(jnp.where(send_hot, route_of[:, None, :], 0), axis=2)
    gate_rows = gate_saved.reshape(tok_rows * top_k, hidden_width)[route_of_slot.reshape(n_slots)]
    gate_rows = gate_rows.reshape(n_peers, slot_cap, hidden_width)
    recv_gate = [
        lax.all_to_all(
            gate_rows[:, :, a:b], "expert", split_axis=0, concat_axis=0, tiled=True
        ).reshape(n_slots, b - a)
        for a, b in zip(gate_cuts, gate_cuts[1:])
    ]

    mine = meta_all[:, :top_k, :] == me.astype(jnp.float32)
    prob_of = jnp.sum(jnp.where(mine, meta_all[:, top_k:, :], 0.0), axis=1)
    recv_hot = slot_onehot(jnp.any(mine, axis=1))
    tok_ids = lax.broadcasted_iota(jnp.int32, (1, 1, tok_rows), 2)
    src = lax.broadcasted_iota(jnp.int32, (n_peers, slot_cap), 0)
    row_of_slot = (src * tok_rows + jnp.sum(jnp.where(recv_hot, tok_ids, 0), axis=2)).reshape(n_slots)
    prob_of_slot = jnp.sum(jnp.where(recv_hot, prob_of[:, None, :], 0.0), axis=2).reshape(n_slots)
    used = jnp.any(recv_hot, axis=2).reshape(n_slots)
    rows_in = jnp.where(used[:, None], rows_all[row_of_slot], 0)
    routed = (prob_of_slot[:, None] * grad_all[row_of_slot].astype(jnp.float32)).astype(jnp.bfloat16)

    shares = []
    hidden, part = [], None
    for j, (a, b) in enumerate(zip(gate_cuts, gate_cuts[1:])):
        up_act = mm(rows_in, up_mat[:, a:b], 1, 0)
        hidden_grad = mm(routed, down_mat[a:b, :], 1, 1)
        gate_val = recv_gate[j].astype(jnp.float32)
        gate_sig = jax.nn.sigmoid(gate_val)
        gate_act = gate_val * gate_sig
        hidden.append((gate_act * up_act).astype(jnp.bfloat16))
        up_grad = (hidden_grad * gate_act).astype(jnp.bfloat16)
        gate_grad = (hidden_grad * up_act * gate_sig * (1.0 + gate_val * (1.0 - gate_sig))).astype(
            jnp.bfloat16
        )
        both = jnp.concatenate([gate_grad, up_grad], axis=1)
        term = mm(rows_in, both, 0, 0).astype(jnp.bfloat16)
        shares.append(lax.psum_scatter(term, "dp", scatter_dimension=0, tiled=True))
        piece = mm(gate_grad, gate_mat[:, a:b], 1, 1) + mm(up_grad, up_mat[:, a:b], 1, 1)
        part = piece if part is None else part + piece
    hidden_act = jnp.concatenate(hidden, axis=1)
    term_down = mm(hidden_act, routed, 0, 0).astype(jnp.bfloat16)
    share_down = lax.psum_scatter(term_down, "dp", scatter_dimension=0, tiled=True)

    back = part.astype(jnp.bfloat16).reshape(n_peers, slot_cap, model_width)
    returned = lax.all_to_all(back, "expert", split_axis=0, concat_axis=0, tiled=True)
    input_grad = mm(
        send_hot.reshape(n_slots, tok_rows).astype(jnp.bfloat16),
        returned.reshape(n_slots, model_width),
        0,
        0,
    ).astype(jnp.bfloat16)

    def scaled(share):
        return (grad_scale * share.astype(jnp.float32)).astype(jnp.bfloat16)

    widths = [b - a for a, b in zip(gate_cuts, gate_cuts[1:])]
    grad_gate = jnp.concatenate([scaled(s[:, :w]) for s, w in zip(shares, widths)], axis=1)[None]
    grad_up = jnp.concatenate([scaled(s[:, w:]) for s, w in zip(shares, widths)], axis=1)[None]
    return (input_grad, grad_gate, grad_up, scaled(share_down)[None])


def solution(mesh):
    return jax.shard_map(
        local,
        mesh=mesh,
        in_specs=(
            P(("dp", "expert"), None),
            P(("dp", "expert"), None),
            P(("dp", "expert"), None, None),
            P(("dp", "expert"), None),
            P(("dp", "expert"), None),
            P("expert", None, None),
            P("expert", None, None),
            P("expert", None, None),
        ),
        out_specs=(
            P(("dp", "expert"), None),
            P("expert", "dp", None),
            P("expert", "dp", None),
            P("expert", "dp", None),
        ),
        check_vma=False,
    )
```

```python
import functools

import jax
import jax.numpy as jnp
from jax import lax
from jax.experimental import pallas as pl
from jax.experimental.pallas import tpu as pltpu
from jax.sharding import PartitionSpec as P

grad_scale = 0.0625
slot_cap = 48
gate_cuts = (0, 640, 1408)


def mm(a, b, ca, cb):
    return lax.dot_general(a, b, (((ca,), (cb,)), ((), ())), preferred_element_type=jnp.float32)


def slot_of_token(chosen):
    n_tok = chosen.shape[1]
    before = (
        lax.broadcasted_iota(jnp.int32, (n_tok, n_tok), 0)
        < lax.broadcasted_iota(jnp.int32, (n_tok, n_tok), 1)
    ).astype(jnp.bfloat16)
    rank = mm(chosen.astype(jnp.bfloat16), before, 1, 0).astype(jnp.int32)
    return jnp.where(chosen, rank, -1)


def pick_kernel(with_prob, slot_ref, prob_ref, own_ref, other_ref, out_ref):
    rows, toks = out_ref.shape[0], own_ref.shape[0]
    hit = lax.broadcasted_iota(jnp.int32, (rows, 2 * toks), 0) == slot_ref[0]
    hot = hit.astype(jnp.float32).astype(jnp.bfloat16)
    got = jnp.dot(hot[:, :toks], own_ref[...], preferred_element_type=jnp.float32)
    got = got + jnp.dot(hot[:, toks:], other_ref[...], preferred_element_type=jnp.float32)
    if with_prob:
        got = got * jnp.sum(jnp.where(hit, prob_ref[0], 0.0), axis=1, keepdims=True)
    out_ref[...] = got.astype(out_ref.dtype)


def pick(slots, probs, own, other, with_prob):
    chips, _, pair = slots.shape
    tok, width = pair // 2, own.shape[1]
    rows = 2 * slot_cap
    small = pl.BlockSpec((1, 1, pair), lambda i: (i, 0, 0))
    big = pl.BlockSpec((tok, width), lambda i: (i, 0))
    return pl.pallas_call(
        functools.partial(pick_kernel, with_prob),
        out_shape=jax.ShapeDtypeStruct((chips * rows, width), jnp.bfloat16),
        grid=(chips,),
        in_specs=[small, small, big, big],
        out_specs=pl.BlockSpec((rows, width), lambda i: (i, 0)),
        compiler_params=pltpu.CompilerParams(vmem_limit_bytes=24 << 20),
        cost_estimate=pl.CostEstimate(
            flops=2 * chips * rows * pair * width, bytes_accessed=4 * chips * pair * width, transcendentals=0
        ),
    )(slots, probs, own, other)


def back_kernel(cuts, *refs):
    n = len(cuts) - 1
    gate_ref, up_ref, out_ref = refs[2 * n :]
    total = None
    for j, (a, b) in enumerate(zip(cuts, cuts[1:])):
        term = mm(refs[j][...], gate_ref[:, a:b], 1, 1) + mm(refs[n + j][...], up_ref[:, a:b], 1, 1)
        total = term if total is None else total + term
    out_ref[...] = total.astype(out_ref.dtype)


def input_parts(grads, gate_mat, up_mat):
    n_slots = grads[0].shape[0]
    width, hidden = gate_mat.shape
    tile = 256
    whole = pl.BlockSpec((width, hidden), lambda i: (0, 0), pipeline_mode=pl.Buffered(1))
    return pl.pallas_call(
        functools.partial(back_kernel, gate_cuts),
        out_shape=jax.ShapeDtypeStruct((n_slots, width), jnp.bfloat16),
        grid=(n_slots // tile,),
        in_specs=[pl.BlockSpec((tile, b.shape[1]), lambda i: (i, 0)) for b in grads] + [whole, whole],
        out_specs=pl.BlockSpec((tile, width), lambda i: (i, 0)),
        compiler_params=pltpu.CompilerParams(vmem_limit_bytes=40 << 20),
        cost_estimate=pl.CostEstimate(
            flops=4 * n_slots * hidden * width, bytes_accessed=4 * hidden * width, transcendentals=0
        ),
    )(*grads, gate_mat, up_mat)


def local(tokens, out_grad, gate_saved, probs, expert_ids, w_gate, w_up, w_down):
    n_peers = lax.axis_size("expert")
    me = lax.axis_index("expert")
    core = me % 2
    tok_rows, model_width = tokens.shape
    top_k = expert_ids.shape[1]
    hidden_width = w_up.shape[2]
    n_slots = n_peers * slot_cap
    n_chips = n_peers // 2
    gate_mat, up_mat, down_mat = w_gate[0], w_up[0], w_down[0]
    same_core = [[2 * i + c for i in range(n_chips)] for c in range(2)]
    swap = [(i, i ^ 1) for i in range(n_peers)]

    meta = jnp.concatenate([expert_ids.T.astype(jnp.float32), probs.T], axis=0)
    meta_all = lax.all_gather(meta, "expert", axis=0, tiled=False)
    grad_own = lax.all_gather(out_grad, "expert", axis=0, tiled=True, axis_index_groups=same_core)
    rows_own = lax.all_gather(tokens, "expert", axis=0, tiled=True, axis_index_groups=same_core)

    ids_t = expert_ids.T
    experts = lax.broadcasted_iota(jnp.int32, (n_peers, 1, 1), 0)
    named = ids_t[None] == experts
    send_slot = slot_of_token(jnp.any(named, axis=1))
    slots = lax.broadcasted_iota(jnp.int32, (1, slot_cap, 1), 1)
    send_hot = send_slot[:, None, :] == slots
    toks = lax.broadcasted_iota(jnp.int32, (1, top_k, tok_rows), 2)
    ks = lax.broadcasted_iota(jnp.int32, (1, top_k, tok_rows), 1)
    route_of = jnp.sum(jnp.where(named, toks * top_k + ks, 0), axis=1)
    route_of_slot = jnp.sum(jnp.where(send_hot, route_of[:, None, :], 0), axis=2)
    route_of_slot, meta_all = lax.optimization_barrier((route_of_slot, meta_all))
    gate_rows = gate_saved.reshape(tok_rows * top_k, hidden_width)[route_of_slot.reshape(n_slots)]
    gate_rows = gate_rows.reshape(n_peers, slot_cap, hidden_width)
    def own_first(x):
        x = x.reshape(n_chips, 2, tok_rows)
        return jnp.where(core == 0, x, x[:, ::-1]).reshape(n_chips, 1, 2 * tok_rows)

    recv_gate = []
    for j, (a, b) in enumerate(zip(gate_cuts, gate_cuts[1:])):
        cut = gate_rows[:, :, a:b]
        if j > 0:
            cut, _ = lax.optimization_barrier((cut, rows_own))
        got = lax.all_to_all(cut, "expert", split_axis=0, concat_axis=0, tiled=True)
        if j == 0:
            got, grad_own = lax.optimization_barrier((got, grad_own))
        recv_gate.append(got.reshape(n_slots, b - a))
    grad_other = lax.ppermute(grad_own, "expert", swap)
    rows_other = lax.ppermute(rows_own, "expert", swap)

    mine = meta_all[:, :top_k, :] == me.astype(jnp.float32)
    prob_of = own_first(jnp.sum(jnp.where(mine, meta_all[:, top_k:, :], 0.0), axis=1))
    recv_slot = slot_of_token(jnp.any(mine, axis=1))
    odd = lax.broadcasted_iota(jnp.int32, recv_slot.shape, 0) % 2
    recv_slot = own_first(jnp.where(recv_slot >= 0, recv_slot + slot_cap * odd, -1))
    routed = pick(recv_slot, prob_of, grad_own, grad_other, True)
    rows_in = pick(recv_slot, prob_of, rows_own, rows_other, False)

    shares, hidden, gate_grads, up_grads = [], [], [], []
    for j, (a, b) in enumerate(zip(gate_cuts, gate_cuts[1:])):
        hidden_grad = mm(routed, down_mat[a:b, :], 1, 1)
        up_act = mm(rows_in, up_mat[:, a:b], 1, 0)
        gate_val = recv_gate[j].astype(jnp.float32)
        gate_sig = jax.nn.sigmoid(gate_val)
        gate_act = gate_val * gate_sig
        hidden.append((gate_act * up_act).astype(jnp.bfloat16))
        up_grad = (hidden_grad * gate_act).astype(jnp.bfloat16)
        gate_grad = (hidden_grad * up_act * gate_sig * (1.0 + gate_val * (1.0 - gate_sig))).astype(
            jnp.bfloat16
        )
        both = jnp.concatenate([gate_grad, up_grad], axis=1)
        gate_grads.append(gate_grad)
        up_grads.append(up_grad)
        term = (grad_scale * mm(rows_in, both, 0, 0)).astype(jnp.bfloat16)
        shares.append(lax.psum_scatter(term, "dp", scatter_dimension=0, tiled=True))

    hidden_act = jnp.concatenate(hidden, axis=1)
    term_down = (grad_scale * mm(hidden_act, routed, 0, 0)).astype(jnp.bfloat16)
    grads, term_down = lax.optimization_barrier((gate_grads + up_grads, term_down))
    grad_down = lax.psum_scatter(term_down, "dp", scatter_dimension=0, tiled=True)

    back = input_parts(grads, gate_mat, up_mat).reshape(n_peers, slot_cap, model_width)
    returned = lax.all_to_all(back, "expert", split_axis=0, concat_axis=0, tiled=True)
    input_grad = mm(
        send_hot.reshape(n_slots, tok_rows).astype(jnp.bfloat16),
        returned.reshape(n_slots, model_width),
        0,
        0,
    ).astype(jnp.bfloat16)

    widths = [b - a for a, b in zip(gate_cuts, gate_cuts[1:])]
    grad_gate = jnp.concatenate([s[:, :w] for s, w in zip(shares, widths)], axis=1)
    grad_up = jnp.concatenate([s[:, w:] for s, w in zip(shares, widths)], axis=1)
    return (input_grad, grad_gate[None], grad_up[None], grad_down[None])


def solution(mesh):
    return jax.shard_map(
        local,
        mesh=mesh,
        in_specs=(
            P(("dp", "expert"), None),
            P(("dp", "expert"), None),
            P(("dp", "expert"), None, None),
            P(("dp", "expert"), None),
            P(("dp", "expert"), None),
            P("expert", None, None),
            P("expert", None, None),
            P("expert", None, None),
        ),
        out_specs=(
            P(("dp", "expert"), None),
            P("expert", "dp", None),
            P("expert", "dp", None),
            P("expert", "dp", None),
        ),
        check_vma=False,
    )
```

```python
import functools

import jax
import jax.numpy as jnp
from jax import lax
from jax.experimental import pallas as pl
from jax.experimental.pallas import tpu as pltpu
from jax.sharding import PartitionSpec as P

grad_scale = 0.0625
slot_cap = 48
gate_cuts = (0, 640, 1408)


def mm(a, b, ca, cb):
    return lax.dot_general(a, b, (((ca,), (cb,)), ((), ())), preferred_element_type=jnp.float32)


def dispatch_kernel(
    first,
    meta_ref,
    tok_hbm,
    grad_hbm,
    gate_hbm,
    rows_out,
    routed_out,
    gate_out,
    late_out,
    held,
    rows_st,
    routed_st,
    gate_vm,
    slots,
    late,
    landed,
    slot_of,
    hot_st,
    load_sem,
    send_sem,
    recv_sem,
    gate_send,
    gate_recv,
    late_sem,
    out_sem,
):
    n = slots.shape[0]
    tok = tok_hbm.shape[0]
    cap = slots.shape[1]
    top_k = gate_hbm.shape[0]
    me = lax.axis_index("expert")
    core = me % 2
    x = (me // 2) % 4
    y = me // 8
    sib = me + 1 - 2 * core

    def place(da, db, c):
        dx = da * (1 - c) + db * c
        dy = da * c + db * (1 - c)
        return (((y + dy) % 4) * 4 + (x + dx) % 4) * 2 + c

    loads = [
        pltpu.make_async_copy(tok_hbm, held.at[me, pl.ds(0, tok)], load_sem.at[0]),
        pltpu.make_async_copy(grad_hbm, held.at[me, pl.ds(tok, tok)], load_sem.at[1]),
        pltpu.make_async_copy(gate_hbm, gate_vm, load_sem.at[2]),
    ]
    for load in loads:
        load.start()

    barrier = pltpu.get_barrier_semaphore()

    @pl.loop(1, n)
    def _(d):
        pl.semaphore_signal(
            barrier, inc=1, device_id={"expert": (me + d) % n}, device_id_type=pl.DeviceIdType.MESH
        )

    pl.semaphore_wait(barrier, n - 1)

    sent = []

    def send(chunk, half, to):
        part = held.at[chunk, pl.ds(half * tok, tok)]
        copy = pltpu.make_async_remote_copy(
            src_ref=part,
            dst_ref=part,
            send_sem=send_sem.at[len(sent)],
            recv_sem=recv_sem.at[chunk, half],
            device_id={"expert": to},
            device_id_type=pl.DeviceIdType.MESH,
        )
        copy.start()
        sent.append(copy)

    def arrive(chunk, half):
        part = held.at[chunk, pl.ds(half * tok, tok)]
        pltpu.make_async_remote_copy(
            src_ref=part,
            dst_ref=part,
            send_sem=send_sem.at[0],
            recv_sem=recv_sem.at[chunk, half],
            device_id={"expert": sib},
            device_id_type=pl.DeviceIdType.MESH,
        ).wait_recv()

    a_up, a_down = place(1, 0, core), place(3, 0, core)
    b_up, b_down = place(0, 1, core), place(0, 3, core)

    for half in range(2):
        loads[half].wait()
        for to in (a_up, a_down, b_up, b_down, sib):
            send(me, half, to)

    ids = meta_ref[0:top_k, :]
    probs = meta_ref[top_k : 2 * top_k, :]
    peers = lax.broadcasted_iota(jnp.int32, (n, tok), 0).astype(jnp.float32)
    chosen = jnp.zeros((n, tok), jnp.float32)
    for k in range(top_k):
        chosen = jnp.where(peers == ids[k : k + 1, :], 1.0, chosen)
    before = (
        lax.broadcasted_iota(jnp.int32, (tok, tok), 0) < lax.broadcasted_iota(jnp.int32, (tok, tok), 1)
    ).astype(jnp.float32)
    rank = jnp.dot(
        chosen.astype(jnp.bfloat16), before.astype(jnp.bfloat16), preferred_element_type=jnp.float32
    )
    slot_of[...] = jnp.where(chosen > 0.0, rank, -1.0)
    loads[2].wait()

    lane = lax.broadcasted_iota(jnp.int32, (cap, tok), 1)
    lane_f = lane.astype(jnp.float32)
    slot_f = lax.broadcasted_iota(jnp.int32, (cap, tok), 0).astype(jnp.float32)
    gang = hot_st.shape[0] // cap

    @pl.loop(0, n // gang)
    def _(g):
        for i in range(gang):
            e = (me + g * gang + i) % n
            e_f = e.astype(jnp.float32)
            hit = jnp.where(slot_f == slot_of[pl.ds(e, 1), :], 1.0, 0.0)
            prob = jnp.zeros((cap, 1), jnp.float32)
            for k in range(top_k):
                hit_k = jnp.where(ids[k : k + 1, :] == e_f, hit, 0.0)
                hot_st[i * cap : (i + 1) * cap, k * tok : (k + 1) * tok] = hit_k.astype(jnp.bfloat16)
                prob = prob + jnp.sum(hit_k * probs[k : k + 1, :], axis=1, keepdims=True)
            used = jnp.sum(hit, axis=1, keepdims=True)
            index = jnp.sum(hit * lane_f, axis=1, keepdims=True) + 255.0 * (1.0 - used)
            hi = prob.astype(jnp.bfloat16).astype(jnp.float32)
            mid = (prob - hi).astype(jnp.bfloat16).astype(jnp.float32)
            low = prob - hi - mid
            info = jnp.where(
                lane == 0, index, jnp.where(lane == 1, hi, jnp.where(lane == 2, mid, low))
            )
            slots[e, :, first : first + tok] = info.astype(jnp.bfloat16)
        got = jnp.dot(
            hot_st[...], gate_vm[...].reshape(top_k * tok, gate_vm.shape[2]), preferred_element_type=jnp.float32
        ).astype(jnp.bfloat16)
        for i in range(gang):
            e = (me + g * gang + i) % n
            slots[e, :, 0:first] = got[i * cap : (i + 1) * cap, :first]
            late[e] = got[i * cap : (i + 1) * cap, first:]

            @pl.when(g * gang + i > 0)
            def _():
                pltpu.make_async_remote_copy(
                    src_ref=slots.at[e],
                    dst_ref=landed.at[me],
                    send_sem=gate_send.at[e],
                    recv_sem=gate_recv.at[me],
                    device_id={"expert": e},
                    device_id_type=pl.DeviceIdType.MESH,
                ).start()

    late_copy = pltpu.make_async_copy(late, late_out, late_sem)
    late_copy.start()
    landed[me] = slots[me]

    def gate_copy(peer):
        return pltpu.make_async_remote_copy(
            src_ref=slots.at[peer],
            dst_ref=landed.at[peer],
            send_sem=gate_send.at[peer],
            recv_sem=gate_recv.at[peer],
            device_id={"expert": peer},
            device_id_type=pl.DeviceIdType.MESH,
        )

    outs = []

    def pick(chunk):
        info = landed[chunk, :, first : first + tok].astype(jnp.float32)
        hot = jnp.where(lane_f == info[:, 0:1], 1.0, 0.0).astype(jnp.bfloat16)
        prob = info[:, 1:2] + info[:, 2:3] + info[:, 3:4]
        rows_st[chunk] = jnp.dot(
            hot, held[chunk, 0:tok, :], preferred_element_type=jnp.float32
        ).astype(jnp.bfloat16)
        routed_st[chunk] = (
            prob * jnp.dot(hot, held[chunk, tok : 2 * tok, :], preferred_element_type=jnp.float32)
        ).astype(jnp.bfloat16)
        number = len(outs)
        copies = (
            pltpu.make_async_copy(rows_st.at[chunk], rows_out.at[chunk], out_sem.at[number]),
            pltpu.make_async_copy(routed_st.at[chunk], routed_out.at[chunk], out_sem.at[n + number]),
            pltpu.make_async_copy(
                landed.at[chunk, :, pl.ds(0, first)], gate_out.at[chunk], out_sem.at[2 * n + number]
            ),
        )
        for copy in copies:
            copy.start()
        outs.append(copies)

    def from_sibling(da, db):
        chunk = place(da, db, 1 - core)
        gate_copy(chunk).wait_recv()
        for half in range(2):
            arrive(chunk, half)
        pick(chunk)

    events = [(3, 0), (1, 0), (0, 3), (0, 1), (2, 0), (0, 2)]
    events += [(da, db) for da in (3, 1, 2) for db in (3, 1, 2)]
    pick(me)
    behind = [(0, 0)]
    for da, db in events:
        chunk = place(da, db, core)
        order = (1, 0) if (da if db == 0 else db) == 1 else (0, 1)
        for half in order:
            arrive(chunk, half)
            if db == 0:
                if da == 3 and half == 0:
                    send(chunk, half, a_up)
                if da == 1 and half == 1:
                    send(chunk, half, a_down)
                send(chunk, half, b_up)
                send(chunk, half, b_down)
            else:
                if db == 3 and half == 0:
                    send(chunk, half, b_up)
                if db == 1 and half == 1:
                    send(chunk, half, b_down)
            send(chunk, half, sib)
        gate_copy(chunk).wait_recv()
        pick(chunk)
        from_sibling(*behind.pop())
        behind.append((da, db))
    from_sibling(*behind.pop())

    for copy in sent:
        copy.wait_send()

    @pl.loop(1, n)
    def _(d):
        gate_copy((me + d) % n).wait_send()

    late_copy.wait()
    for copies in outs:
        for copy in copies:
            copy.wait()


def dispatch(meta, tokens, out_grad, gate_by_k):
    n = lax.axis_size("expert")
    tok, width = tokens.shape
    top_k, _, hidden = gate_by_k.shape
    first = gate_cuts[1]
    bf16 = jnp.bfloat16
    anywhere = pl.BlockSpec(memory_space=pl.ANY)
    return pl.pallas_call(
        functools.partial(dispatch_kernel, first),
        out_shape=(
            jax.ShapeDtypeStruct((n, slot_cap, width), bf16),
            jax.ShapeDtypeStruct((n, slot_cap, width), bf16),
            jax.ShapeDtypeStruct((n, slot_cap, first), bf16),
            jax.ShapeDtypeStruct((n, slot_cap, hidden - first), bf16),
        ),
        in_specs=[pl.BlockSpec(memory_space=pltpu.VMEM), anywhere, anywhere, anywhere],
        out_specs=(anywhere,) * 4,
        scratch_shapes=[
            pltpu.VMEM((n, 2 * tok, width), bf16),
            pltpu.VMEM((n, slot_cap, width), bf16),
            pltpu.VMEM((n, slot_cap, width), bf16),
            pltpu.VMEM((top_k, tok, hidden), bf16),
            pltpu.VMEM((n, slot_cap, first + tok), bf16),
            pltpu.VMEM((n, slot_cap, hidden - first), bf16),
            pltpu.VMEM((n, slot_cap, first + tok), bf16),
            pltpu.VMEM((n, tok), jnp.float32),
            pltpu.VMEM((4 * slot_cap, top_k * tok), bf16),
            pltpu.SemaphoreType.DMA((3,)),
            pltpu.SemaphoreType.DMA((64,)),
            pltpu.SemaphoreType.DMA((n, 2)),
            pltpu.SemaphoreType.DMA((n,)),
            pltpu.SemaphoreType.DMA((n,)),
            pltpu.SemaphoreType.DMA,
            pltpu.SemaphoreType.DMA((3 * n,)),
        ],
        compiler_params=pltpu.CompilerParams(
            collective_id=0, has_side_effects=True, vmem_limit_bytes=62 << 20
        ),
        cost_estimate=pl.CostEstimate(
            flops=8 * n * slot_cap * tok * width, bytes_accessed=100 << 20, transcendentals=0
        ),
    )(meta, tokens, out_grad, gate_by_k)


def back_kernel(cuts, *refs):
    n = len(cuts) - 1
    gate_ref, up_ref, out_ref = refs[2 * n :]
    total = None
    for j, (a, b) in enumerate(zip(cuts, cuts[1:])):
        term = mm(refs[j][...], gate_ref[:, a:b], 1, 1) + mm(refs[n + j][...], up_ref[:, a:b], 1, 1)
        total = term if total is None else total + term
    out_ref[...] = total.astype(out_ref.dtype)


def input_parts(grads, gate_mat, up_mat):
    n_slots = grads[0].shape[0]
    width, hidden = gate_mat.shape
    tile = 256
    whole = pl.BlockSpec((width, hidden), lambda i: (0, 0), pipeline_mode=pl.Buffered(1))
    return pl.pallas_call(
        functools.partial(back_kernel, gate_cuts),
        out_shape=jax.ShapeDtypeStruct((n_slots, width), jnp.bfloat16),
        grid=(n_slots // tile,),
        in_specs=[pl.BlockSpec((tile, b.shape[1]), lambda i: (i, 0)) for b in grads] + [whole, whole],
        out_specs=pl.BlockSpec((tile, width), lambda i: (i, 0)),
        compiler_params=pltpu.CompilerParams(vmem_limit_bytes=40 << 20),
        cost_estimate=pl.CostEstimate(
            flops=4 * n_slots * hidden * width, bytes_accessed=4 * hidden * width, transcendentals=0
        ),
    )(*grads, gate_mat, up_mat)


def local(tokens, out_grad, gate_saved, probs, expert_ids, w_gate, w_up, w_down):
    n_peers = lax.axis_size("expert")
    tok_rows, model_width = tokens.shape
    top_k = expert_ids.shape[1]
    n_slots = n_peers * slot_cap
    gate_mat, up_mat, down_mat = w_gate[0], w_up[0], w_down[0]

    ids_t = expert_ids.T
    meta = jnp.concatenate(
        [ids_t.astype(jnp.float32), probs.T, jnp.zeros((16 - 2 * top_k, tok_rows), jnp.float32)], axis=0
    )
    rows_in, routed, gate_first, gate_late = dispatch(
        meta, tokens, out_grad, jnp.transpose(gate_saved, (1, 0, 2))
    )
    rows_in = rows_in.reshape(n_slots, model_width)
    routed = routed.reshape(n_slots, model_width)
    gate_late = lax.all_to_all(gate_late, "expert", split_axis=0, concat_axis=0, tiled=True)
    recv_gate = [g.reshape(n_slots, g.shape[2]) for g in (gate_first, gate_late)]

    experts = lax.broadcasted_iota(jnp.int32, (n_peers, 1, 1), 0)
    chosen = jnp.any(ids_t[None] == experts, axis=1)
    before = (
        lax.broadcasted_iota(jnp.int32, (tok_rows, tok_rows), 0)
        < lax.broadcasted_iota(jnp.int32, (tok_rows, tok_rows), 1)
    ).astype(jnp.bfloat16)
    rank = mm(chosen.astype(jnp.bfloat16), before, 1, 0).astype(jnp.int32)
    slots = lax.broadcasted_iota(jnp.int32, (1, slot_cap, 1), 1)
    send_hot = (rank[:, None, :] == slots) & chosen[:, None, :]

    shares, hidden, gate_grads, up_grads = [], [], [], []
    for j, (a, b) in enumerate(zip(gate_cuts, gate_cuts[1:])):
        hidden_grad = mm(routed, down_mat[a:b, :], 1, 1)
        up_act = mm(rows_in, up_mat[:, a:b], 1, 0)
        gate_val = recv_gate[j].astype(jnp.float32)
        gate_sig = jax.nn.sigmoid(gate_val)
        gate_act = gate_val * gate_sig
        hidden.append((gate_act * up_act).astype(jnp.bfloat16))
        up_grad = (hidden_grad * gate_act).astype(jnp.bfloat16)
        gate_grad = (hidden_grad * up_act * gate_sig * (1.0 + gate_val * (1.0 - gate_sig))).astype(
            jnp.bfloat16
        )
        both = jnp.concatenate([gate_grad, up_grad], axis=1)
        gate_grads.append(gate_grad)
        up_grads.append(up_grad)
        term = (grad_scale * mm(rows_in, both, 0, 0)).astype(jnp.bfloat16)
        shares.append(lax.psum_scatter(term, "dp", scatter_dimension=0, tiled=True))

    hidden_act = jnp.concatenate(hidden, axis=1)
    term_down = (grad_scale * mm(hidden_act, routed, 0, 0)).astype(jnp.bfloat16)
    grads, term_down = lax.optimization_barrier((gate_grads + up_grads, term_down))
    grad_down = lax.psum_scatter(term_down, "dp", scatter_dimension=0, tiled=True)

    back = input_parts(grads, gate_mat, up_mat).reshape(n_peers, slot_cap, model_width)
    returned = lax.all_to_all(back, "expert", split_axis=0, concat_axis=0, tiled=True)
    input_grad = mm(
        send_hot.reshape(n_slots, tok_rows).astype(jnp.bfloat16),
        returned.reshape(n_slots, model_width),
        0,
        0,
    ).astype(jnp.bfloat16)

    widths = [b - a for a, b in zip(gate_cuts, gate_cuts[1:])]
    grad_gate = jnp.concatenate([s[:, :w] for s, w in zip(shares, widths)], axis=1)
    grad_up = jnp.concatenate([s[:, w:] for s, w in zip(shares, widths)], axis=1)
    return (input_grad, grad_gate[None], grad_up[None], grad_down[None])


def solution(mesh):
    return jax.shard_map(
        local,
        mesh=mesh,
        in_specs=(
            P(("dp", "expert"), None),
            P(("dp", "expert"), None),
            P(("dp", "expert"), None, None),
            P(("dp", "expert"), None),
            P(("dp", "expert"), None),
            P("expert", None, None),
            P("expert", None, None),
            P("expert", None, None),
        ),
        out_specs=(
            P(("dp", "expert"), None),
            P("expert", "dp", None),
            P("expert", "dp", None),
            P("expert", "dp", None),
        ),
        check_vma=False,
    )
```

```python
import functools

import jax
import jax.numpy as jnp
from jax import lax
from jax.experimental import pallas as pl
from jax.experimental.pallas import tpu as pltpu
from jax.sharding import PartitionSpec as P

grad_scale = 0.0625
slot_cap = 48
gate_cuts = (0, 768, 1408)
pieces = 2
early_gates = 9


def mm(a, b, ca, cb):
    return lax.dot_general(a, b, (((ca,), (cb,)), ((), ())), preferred_element_type=jnp.float32)


def dispatch_kernel(
    first,
    meta_ref,
    tok_hbm,
    grad_hbm,
    gate_hbm,
    rows_out,
    routed_out,
    gate_out,
    late_out,
    held,
    rows_st,
    routed_st,
    gate_vm,
    slots,
    late,
    landed,
    slot_of,
    hot_st,
    load_sem,
    send_sem,
    recv_sem,
    gate_send,
    gate_recv,
    late_sem,
    out_sem,
):
    n = slots.shape[0]
    tok = tok_hbm.shape[0]
    cap = slots.shape[1]
    top_k = gate_hbm.shape[0]
    me = lax.axis_index("expert")
    core = me % 2
    x = (me // 2) % 4
    y = me // 8
    sib = me + 1 - 2 * core

    def place(da, db, c):
        dx = da * (1 - c) + db * c
        dy = da * c + db * (1 - c)
        return (((y + dy) % 4) * 4 + (x + dx) % 4) * 2 + c

    loads = [
        pltpu.make_async_copy(tok_hbm, held.at[me, pl.ds(0, tok)], load_sem.at[0]),
        pltpu.make_async_copy(grad_hbm, held.at[me, pl.ds(tok, tok)], load_sem.at[1]),
        pltpu.make_async_copy(gate_hbm, gate_vm, load_sem.at[2]),
    ]
    for load in loads:
        load.start()

    barrier = pltpu.get_barrier_semaphore()

    @pl.loop(1, n)
    def _(d):
        pl.semaphore_signal(
            barrier, inc=1, device_id={"expert": (me + d) % n}, device_id_type=pl.DeviceIdType.MESH
        )

    pl.semaphore_wait(barrier, n - 1)

    sent = []

    piece = held.shape[1] // pieces

    def send(chunk, number, to):
        part = held.at[chunk, pl.ds(number * piece, piece)]
        copy = pltpu.make_async_remote_copy(
            src_ref=part,
            dst_ref=part,
            send_sem=send_sem.at[len(sent)],
            recv_sem=recv_sem.at[chunk, number],
            device_id={"expert": to},
            device_id_type=pl.DeviceIdType.MESH,
        )
        copy.start()
        sent.append(copy)

    def arrive(chunk, number):
        part = held.at[chunk, pl.ds(number * piece, piece)]
        pltpu.make_async_remote_copy(
            src_ref=part,
            dst_ref=part,
            send_sem=send_sem.at[0],
            recv_sem=recv_sem.at[chunk, number],
            device_id={"expert": sib},
            device_id_type=pl.DeviceIdType.MESH,
        ).wait_recv()

    a_up, a_down = place(1, 0, core), place(3, 0, core)
    b_up, b_down = place(0, 1, core), place(0, 3, core)

    for number in range(pieces):
        if number % (pieces // 2) == 0:
            loads[number // (pieces // 2)].wait()
        for to in (a_up, a_down, b_up, b_down, sib):
            send(me, number, to)

    ids = meta_ref[0:top_k, :]
    probs = meta_ref[top_k : 2 * top_k, :]
    peers = lax.broadcasted_iota(jnp.int32, (n, tok), 0).astype(jnp.float32)
    chosen = jnp.zeros((n, tok), jnp.float32)
    for k in range(top_k):
        chosen = jnp.where(peers == ids[k : k + 1, :], 1.0, chosen)
    before = (
        lax.broadcasted_iota(jnp.int32, (tok, tok), 0) < lax.broadcasted_iota(jnp.int32, (tok, tok), 1)
    ).astype(jnp.float32)
    rank = jnp.dot(
        chosen.astype(jnp.bfloat16), before.astype(jnp.bfloat16), preferred_element_type=jnp.float32
    )
    slot_of[...] = jnp.where(chosen > 0.0, rank, -1.0)
    loads[2].wait()

    lane = lax.broadcasted_iota(jnp.int32, (cap, tok), 1)
    lane_f = lane.astype(jnp.float32)
    slot_f = lax.broadcasted_iota(jnp.int32, (cap, tok), 0).astype(jnp.float32)
    gang = hot_st.shape[0] // cap

    @pl.loop(0, n // gang)
    def _(g):
        for i in range(gang):
            e = (me + g * gang + i) % n
            e_f = e.astype(jnp.float32)
            hit = jnp.where(slot_f == slot_of[pl.ds(e, 1), :], 1.0, 0.0)
            prob = jnp.zeros((cap, 1), jnp.float32)
            for k in range(top_k):
                hit_k = jnp.where(ids[k : k + 1, :] == e_f, hit, 0.0)
                hot_st[i * cap : (i + 1) * cap, k * tok : (k + 1) * tok] = hit_k.astype(jnp.bfloat16)
                prob = prob + jnp.sum(hit_k * probs[k : k + 1, :], axis=1, keepdims=True)
            used = jnp.sum(hit, axis=1, keepdims=True)
            index = jnp.sum(hit * lane_f, axis=1, keepdims=True) + 255.0 * (1.0 - used)
            hi = prob.astype(jnp.bfloat16).astype(jnp.float32)
            mid = (prob - hi).astype(jnp.bfloat16).astype(jnp.float32)
            low = prob - hi - mid
            info = jnp.where(
                lane == 0, index, jnp.where(lane == 1, hi, jnp.where(lane == 2, mid, low))
            )
            slots[e, :, first : first + tok] = info.astype(jnp.bfloat16)
        got = jnp.dot(
            hot_st[...], gate_vm[...].reshape(top_k * tok, gate_vm.shape[2]), preferred_element_type=jnp.float32
        ).astype(jnp.bfloat16)
        for i in range(gang):
            e = (me + g * gang + i) % n
            slots[e, :, 0:first] = got[i * cap : (i + 1) * cap, :first]
            late[e] = got[i * cap : (i + 1) * cap, first:]

    late_copy = pltpu.make_async_copy(late, late_out, late_sem)
    late_copy.start()
    landed[me] = slots[me]
    events = [(3, 0), (1, 0), (0, 3), (0, 1), (2, 0), (0, 2)]
    events += [(da, db) for da in (3, 1, 2) for db in (3, 1, 2)]
    to_send = [(0, 0, 1)] + [(4 - da, 4 - db, flip) for da, db in events for flip in range(2)]

    def gate_sends(count):
        for da, db, flip in to_send[:count]:
            e = place(da, db, core) + flip * (1 - 2 * core)
            pltpu.make_async_remote_copy(
                src_ref=slots.at[e],
                dst_ref=landed.at[me],
                send_sem=gate_send.at[e],
                recv_sem=gate_recv.at[me],
                device_id={"expert": e},
                device_id_type=pl.DeviceIdType.MESH,
            ).start()
        del to_send[:count]

    gate_sends(early_gates)

    def gate_copy(peer):
        return pltpu.make_async_remote_copy(
            src_ref=slots.at[peer],
            dst_ref=landed.at[peer],
            send_sem=gate_send.at[peer],
            recv_sem=gate_recv.at[peer],
            device_id={"expert": peer},
            device_id_type=pl.DeviceIdType.MESH,
        )

    outs = []

    def pick(chunk):
        info = landed[chunk, :, first : first + tok].astype(jnp.float32)
        hot = jnp.where(lane_f == info[:, 0:1], 1.0, 0.0).astype(jnp.bfloat16)
        prob = info[:, 1:2] + info[:, 2:3] + info[:, 3:4]
        rows_st[chunk] = jnp.dot(
            hot, held[chunk, 0:tok, :], preferred_element_type=jnp.float32
        ).astype(jnp.bfloat16)
        routed_st[chunk] = (
            prob * jnp.dot(hot, held[chunk, tok : 2 * tok, :], preferred_element_type=jnp.float32)
        ).astype(jnp.bfloat16)
        number = len(outs)
        copies = (
            pltpu.make_async_copy(rows_st.at[chunk], rows_out.at[chunk], out_sem.at[number]),
            pltpu.make_async_copy(routed_st.at[chunk], routed_out.at[chunk], out_sem.at[n + number]),
            pltpu.make_async_copy(
                landed.at[chunk, :, pl.ds(0, first)], gate_out.at[chunk], out_sem.at[2 * n + number]
            ),
        )
        for copy in copies:
            copy.start()
        outs.append(copies)

    def from_sibling(da, db):
        chunk = place(da, db, 1 - core)
        gate_copy(chunk).wait_recv()
        for number in range(pieces):
            arrive(chunk, number)
        pick(chunk)

    pick(me)
    behind = [(0, 0)]
    for da, db in events:
        chunk = place(da, db, core)
        low, high = range(pieces // 2), range(pieces // 2, pieces)
        side = da if db == 0 else db
        for number in (*high, *low) if side == 1 else (*low, *high):
            arrive(chunk, number)
            up, down = (a_up, a_down) if db == 0 else (b_up, b_down)
            if side == 3 and number in low:
                send(chunk, number, up)
            if side == 1 and number in high:
                send(chunk, number, down)
            if db == 0:
                send(chunk, number, b_up)
                send(chunk, number, b_down)
            send(chunk, number, sib)
        gate_sends(2)
        gate_copy(chunk).wait_recv()
        pick(chunk)
        from_sibling(*behind.pop())
        behind.append((da, db))
    from_sibling(*behind.pop())

    for copy in sent:
        copy.wait_send()

    @pl.loop(1, n)
    def _(d):
        gate_copy((me + d) % n).wait_send()

    late_copy.wait()
    for copies in outs:
        for copy in copies:
            copy.wait()


def dispatch(meta, tokens, out_grad, gate_by_k):
    n = lax.axis_size("expert")
    tok, width = tokens.shape
    top_k, _, hidden = gate_by_k.shape
    first = gate_cuts[1]
    bf16 = jnp.bfloat16
    anywhere = pl.BlockSpec(memory_space=pl.ANY)
    return pl.pallas_call(
        functools.partial(dispatch_kernel, first),
        out_shape=(
            jax.ShapeDtypeStruct((n, slot_cap, width), bf16),
            jax.ShapeDtypeStruct((n, slot_cap, width), bf16),
            jax.ShapeDtypeStruct((n, slot_cap, first), bf16),
            jax.ShapeDtypeStruct((n, slot_cap, hidden - first), bf16),
        ),
        in_specs=[pl.BlockSpec(memory_space=pltpu.VMEM), anywhere, anywhere, anywhere],
        out_specs=(anywhere,) * 4,
        scratch_shapes=[
            pltpu.VMEM((n, 2 * tok, width), bf16),
            pltpu.VMEM((n, slot_cap, width), bf16),
            pltpu.VMEM((n, slot_cap, width), bf16),
            pltpu.VMEM((top_k, tok, hidden), bf16),
            pltpu.VMEM((n, slot_cap, first + tok), bf16),
            pltpu.VMEM((n, slot_cap, hidden - first), bf16),
            pltpu.VMEM((n, slot_cap, first + tok), bf16),
            pltpu.VMEM((n, tok), jnp.float32),
            pltpu.VMEM((4 * slot_cap, top_k * tok), bf16),
            pltpu.SemaphoreType.DMA((3,)),
            pltpu.SemaphoreType.DMA((31 * pieces,)),
            pltpu.SemaphoreType.DMA((n, pieces)),
            pltpu.SemaphoreType.DMA((n,)),
            pltpu.SemaphoreType.DMA((n,)),
            pltpu.SemaphoreType.DMA,
            pltpu.SemaphoreType.DMA((3 * n,)),
        ],
        compiler_params=pltpu.CompilerParams(
            collective_id=0, has_side_effects=True, vmem_limit_bytes=62 << 20
        ),
        cost_estimate=pl.CostEstimate(
            flops=8 * n * slot_cap * tok * width, bytes_accessed=100 << 20, transcendentals=0
        ),
    )(meta, tokens, out_grad, gate_by_k)


def back_kernel(cuts, *refs):
    n = len(cuts) - 1
    gate_ref, up_ref, out_ref = refs[2 * n :]
    total = None
    for j, (a, b) in enumerate(zip(cuts, cuts[1:])):
        term = mm(refs[j][...], gate_ref[:, a:b], 1, 1) + mm(refs[n + j][...], up_ref[:, a:b], 1, 1)
        total = term if total is None else total + term
    out_ref[...] = total.astype(out_ref.dtype)


def input_parts(grads, gate_mat, up_mat):
    n_slots = grads[0].shape[0]
    width, hidden = gate_mat.shape
    tile = 256
    whole = pl.BlockSpec((width, hidden), lambda i: (0, 0), pipeline_mode=pl.Buffered(1))
    return pl.pallas_call(
        functools.partial(back_kernel, gate_cuts),
        out_shape=jax.ShapeDtypeStruct((n_slots, width), jnp.bfloat16),
        grid=(n_slots // tile,),
        in_specs=[pl.BlockSpec((tile, b.shape[1]), lambda i: (i, 0)) for b in grads] + [whole, whole],
        out_specs=pl.BlockSpec((tile, width), lambda i: (i, 0)),
        compiler_params=pltpu.CompilerParams(vmem_limit_bytes=40 << 20),
        cost_estimate=pl.CostEstimate(
            flops=4 * n_slots * hidden * width, bytes_accessed=4 * hidden * width, transcendentals=0
        ),
    )(*grads, gate_mat, up_mat)


def reduce_kernel(
    rows_ref,
    routed_ref,
    gate_ref,
    up_ref,
    hidden_ref,
    gate_out,
    up_out,
    down_out,
    wide,
    tall,
    wide_first,
    tall_first,
    wide_send,
    wide_recv,
    tall_send,
    tall_recv,
):
    n = hidden_ref.shape[0]
    me = lax.axis_index("dp")
    quarter = gate_out.shape[0]
    half = tall_first.shape[2]
    ahead, behind = (me + 1) % n, (me + n - 1) % n

    barrier = pltpu.get_barrier_semaphore()
    for to in (ahead, behind):
        pl.semaphore_signal(
            barrier, inc=1, device_id={"dp": to}, device_id_type=pl.DeviceIdType.MESH
        )
    pl.semaphore_wait(barrier, 2)

    def copy_of(which, way, hop):
        first, landed, send_sem, recv_sem = (
            (wide_first, wide, wide_send, wide_recv) if which == 0 else (tall_first, tall, tall_send, tall_recv)
        )
        return pltpu.make_async_remote_copy(
            src_ref=first.at[way] if hop == 0 else landed.at[way, hop - 1],
            dst_ref=landed.at[way, hop],
            send_sem=send_sem.at[way, hop],
            recv_sem=recv_sem.at[way, hop],
            device_id={"dp": ahead if way == 0 else behind},
            device_id_type=pl.DeviceIdType.MESH,
        )

    def term(which, way, share):
        if which == 0:
            columns = pl.ds(pl.multiple_of(share * quarter, quarter), quarter)
            got = mm(rows_ref[:, columns], (gate_ref if way == 0 else up_ref)[...], 0, 0)
        else:
            got = mm(hidden_ref[share], routed_ref[:, way * half : (way + 1) * half], 0, 0)
        return grad_scale * got

    for hop in range(n):
        for which in range(2):
            for way in range(2):
                share = (me + n - 1 - hop) % n if way == 0 else (me + 1 + hop) % n
                part = term(which, way, share)
                if hop == 0:
                    first = wide_first if which == 0 else tall_first
                    first[way] = part.astype(jnp.bfloat16)
                else:
                    landed = wide if which == 0 else tall
                    copy_of(which, way, hop - 1).wait_recv()
                    part = (part + landed[way, hop - 1].astype(jnp.float32)).astype(jnp.bfloat16)
                    if hop < n - 1:
                        landed[way, hop - 1] = part
                    elif which == 0:
                        (gate_out if way == 0 else up_out)[...] = part
                    else:
                        down_out[:, way * half : (way + 1) * half] = part
                if hop < n - 1:
                    copy_of(which, way, hop).start()
    for hop in range(n - 1):
        for which in range(2):
            for way in range(2):
                copy_of(which, way, hop).wait_send()


def reduce_late(rows_in, routed, gate_grad, up_grad, hidden_parts):
    n = lax.axis_size("dp")
    slots, width = rows_in.shape
    cols = gate_grad.shape[1]
    tall_rows = hidden_parts.shape[2]
    quarter, half = width // n, width // 2
    bf16 = jnp.bfloat16
    vmem = pl.BlockSpec(memory_space=pltpu.VMEM)
    return pl.pallas_call(
        reduce_kernel,
        out_shape=(
            jax.ShapeDtypeStruct((quarter, cols), bf16),
            jax.ShapeDtypeStruct((quarter, cols), bf16),
            jax.ShapeDtypeStruct((tall_rows, width), bf16),
        ),
        in_specs=[vmem] * 5,
        out_specs=(vmem,) * 3,
        scratch_shapes=[
            pltpu.VMEM((2, n - 1, quarter, cols), bf16),
            pltpu.VMEM((2, n - 1, tall_rows, half), bf16),
            pltpu.VMEM((2, quarter, cols), bf16),
            pltpu.VMEM((2, tall_rows, half), bf16),
            pltpu.SemaphoreType.DMA((2, n - 1)),
            pltpu.SemaphoreType.DMA((2, n - 1)),
            pltpu.SemaphoreType.DMA((2, n - 1)),
            pltpu.SemaphoreType.DMA((2, n - 1)),
        ],
        compiler_params=pltpu.CompilerParams(
            collective_id=1, has_side_effects=True, vmem_limit_bytes=56 << 20
        ),
        cost_estimate=pl.CostEstimate(
            flops=2 * slots * width * (2 * cols + n * tall_rows), bytes_accessed=300 << 20, transcendentals=0
        ),
    )(rows_in, routed, gate_grad, up_grad, hidden_parts)


def local(tokens, out_grad, gate_saved, probs, expert_ids, w_gate, w_up, w_down):
    n_peers = lax.axis_size("expert")
    tok_rows, model_width = tokens.shape
    top_k = expert_ids.shape[1]
    n_slots = n_peers * slot_cap
    gate_mat, up_mat, down_mat = w_gate[0], w_up[0], w_down[0]

    ids_t = expert_ids.T
    meta = jnp.concatenate(
        [ids_t.astype(jnp.float32), probs.T, jnp.zeros((16 - 2 * top_k, tok_rows), jnp.float32)], axis=0
    )
    rows_in, routed, gate_first, gate_late = dispatch(
        meta, tokens, out_grad, jnp.transpose(gate_saved, (1, 0, 2))
    )
    rows_in = rows_in.reshape(n_slots, model_width)
    routed = routed.reshape(n_slots, model_width)
    gate_late = lax.all_to_all(gate_late, "expert", split_axis=0, concat_axis=0, tiled=True)
    recv_gate = [g.reshape(n_slots, g.shape[2]) for g in (gate_first, gate_late)]

    experts = lax.broadcasted_iota(jnp.int32, (n_peers, 1, 1), 0)
    chosen = jnp.any(ids_t[None] == experts, axis=1)
    before = (
        lax.broadcasted_iota(jnp.int32, (tok_rows, tok_rows), 0)
        < lax.broadcasted_iota(jnp.int32, (tok_rows, tok_rows), 1)
    ).astype(jnp.bfloat16)
    rank = mm(chosen.astype(jnp.bfloat16), before, 1, 0).astype(jnp.int32)
    slots = lax.broadcasted_iota(jnp.int32, (1, slot_cap, 1), 1)
    send_hot = (rank[:, None, :] == slots) & chosen[:, None, :]

    hidden, gate_grads, up_grads, first_share = [], [], [], None
    for j, (a, b) in enumerate(zip(gate_cuts, gate_cuts[1:])):
        hidden_grad = mm(routed, down_mat[a:b, :], 1, 1)
        up_act = mm(rows_in, up_mat[:, a:b], 1, 0)
        gate_val = recv_gate[j].astype(jnp.float32)
        gate_sig = jax.nn.sigmoid(gate_val)
        gate_act = gate_val * gate_sig
        hidden.append((gate_act * up_act).astype(jnp.bfloat16))
        up_grad = (hidden_grad * gate_act).astype(jnp.bfloat16)
        gate_grad = (hidden_grad * up_act * gate_sig * (1.0 + gate_val * (1.0 - gate_sig))).astype(
            jnp.bfloat16
        )
        gate_grads.append(gate_grad)
        up_grads.append(up_grad)
        if j == 0:
            both = jnp.concatenate([gate_grad, up_grad], axis=1)
            term = (grad_scale * mm(rows_in, both, 0, 0)).astype(jnp.bfloat16)
            first_share = lax.psum_scatter(term, "dp", scatter_dimension=0, tiled=True)

    back = input_parts(gate_grads + up_grads, gate_mat, up_mat)
    n_dp = lax.axis_size("dp")
    hidden_parts = jnp.concatenate(hidden, axis=1).reshape(n_slots, n_dp, -1).transpose(1, 0, 2)
    back, hidden_parts = lax.optimization_barrier((back, hidden_parts))
    late_gate, late_up, grad_down = reduce_late(rows_in, routed, gate_grads[1], up_grads[1], hidden_parts)

    back = back.reshape(n_peers, slot_cap, model_width)
    returned = lax.all_to_all(back, "expert", split_axis=0, concat_axis=0, tiled=True)
    input_grad = mm(
        send_hot.reshape(n_slots, tok_rows).astype(jnp.bfloat16),
        returned.reshape(n_slots, model_width),
        0,
        0,
    ).astype(jnp.bfloat16)

    first = gate_cuts[1]
    grad_gate = jnp.concatenate([first_share[:, :first], late_gate], axis=1)
    grad_up = jnp.concatenate([first_share[:, first:], late_up], axis=1)
    return (input_grad, grad_gate[None], grad_up[None], grad_down[None])


def solution(mesh):
    return jax.shard_map(
        local,
        mesh=mesh,
        in_specs=(
            P(("dp", "expert"), None),
            P(("dp", "expert"), None),
            P(("dp", "expert"), None, None),
            P(("dp", "expert"), None),
            P(("dp", "expert"), None),
            P("expert", None, None),
            P("expert", None, None),
            P("expert", None, None),
        ),
        out_specs=(
            P(("dp", "expert"), None),
            P("expert", "dp", None),
            P("expert", "dp", None),
            P("expert", "dp", None),
        ),
        check_vma=False,
    )
```

```python
import functools

import jax
import jax.numpy as jnp
from jax import lax
from jax.experimental import pallas as pl
from jax.experimental.pallas import tpu as pltpu
from jax.sharding import PartitionSpec as P

grad_scale = 0.0625
slot_cap = 48
gate_cuts = (0, 768, 1408)
pieces = 2
early_gates = 9


def mm(a, b, ca, cb):
    return lax.dot_general(a, b, (((ca,), (cb,)), ((), ())), preferred_element_type=jnp.float32)


def dispatch_kernel(
    first,
    meta_ref,
    tok_hbm,
    grad_hbm,
    gate_hbm,
    rows_out,
    routed_out,
    gate_out,
    late_out,
    held,
    rows_st,
    routed_st,
    gate_vm,
    slots,
    late,
    landed,
    slot_of,
    hot_st,
    load_sem,
    send_sem,
    recv_sem,
    gate_send,
    gate_recv,
    late_sem,
    out_sem,
):
    n = slots.shape[0]
    tok = tok_hbm.shape[0]
    cap = slots.shape[1]
    top_k = gate_hbm.shape[0]
    me = lax.axis_index("expert")
    core = me % 2
    x = (me // 2) % 4
    y = me // 8
    sib = me + 1 - 2 * core

    def place(da, db, c):
        dx = da * (1 - c) + db * c
        dy = da * c + db * (1 - c)
        return (((y + dy) % 4) * 4 + (x + dx) % 4) * 2 + c

    loads = [
        pltpu.make_async_copy(tok_hbm, held.at[me, pl.ds(0, tok)], load_sem.at[0]),
        pltpu.make_async_copy(grad_hbm, held.at[me, pl.ds(tok, tok)], load_sem.at[1]),
        pltpu.make_async_copy(gate_hbm, gate_vm, load_sem.at[2]),
    ]
    for load in loads:
        load.start()

    barrier = pltpu.get_barrier_semaphore()

    @pl.loop(1, n)
    def _(d):
        pl.semaphore_signal(
            barrier, inc=1, device_id={"expert": (me + d) % n}, device_id_type=pl.DeviceIdType.MESH
        )

    pl.semaphore_wait(barrier, n - 1)

    sent = []

    piece = held.shape[1] // pieces

    def send(chunk, number, to):
        part = held.at[chunk, pl.ds(number * piece, piece)]
        copy = pltpu.make_async_remote_copy(
            src_ref=part,
            dst_ref=part,
            send_sem=send_sem.at[len(sent)],
            recv_sem=recv_sem.at[chunk, number],
            device_id={"expert": to},
            device_id_type=pl.DeviceIdType.MESH,
        )
        copy.start()
        sent.append(copy)

    def arrive(chunk, number):
        part = held.at[chunk, pl.ds(number * piece, piece)]
        pltpu.make_async_remote_copy(
            src_ref=part,
            dst_ref=part,
            send_sem=send_sem.at[0],
            recv_sem=recv_sem.at[chunk, number],
            device_id={"expert": sib},
            device_id_type=pl.DeviceIdType.MESH,
        ).wait_recv()

    a_up, a_down = place(1, 0, core), place(3, 0, core)
    b_up, b_down = place(0, 1, core), place(0, 3, core)

    for number in range(pieces):
        if number % (pieces // 2) == 0:
            loads[number // (pieces // 2)].wait()
        for to in (a_up, a_down, b_up, b_down, sib):
            send(me, number, to)

    ids = meta_ref[0:top_k, :]
    probs = meta_ref[top_k : 2 * top_k, :]
    peers = lax.broadcasted_iota(jnp.int32, (n, tok), 0).astype(jnp.float32)
    chosen = jnp.zeros((n, tok), jnp.float32)
    for k in range(top_k):
        chosen = jnp.where(peers == ids[k : k + 1, :], 1.0, chosen)
    before = (
        lax.broadcasted_iota(jnp.int32, (tok, tok), 0) < lax.broadcasted_iota(jnp.int32, (tok, tok), 1)
    ).astype(jnp.float32)
    rank = jnp.dot(
        chosen.astype(jnp.bfloat16), before.astype(jnp.bfloat16), preferred_element_type=jnp.float32
    )
    slot_of[...] = jnp.where(chosen > 0.0, rank, -1.0)
    loads[2].wait()

    lane = lax.broadcasted_iota(jnp.int32, (cap, tok), 1)
    lane_f = lane.astype(jnp.float32)
    slot_f = lax.broadcasted_iota(jnp.int32, (cap, tok), 0).astype(jnp.float32)
    gang = hot_st.shape[0] // cap

    @pl.loop(0, n // gang)
    def _(g):
        for i in range(gang):
            e = (me + g * gang + i) % n
            e_f = e.astype(jnp.float32)
            hit = jnp.where(slot_f == slot_of[pl.ds(e, 1), :], 1.0, 0.0)
            prob = jnp.zeros((cap, 1), jnp.float32)
            for k in range(top_k):
                hit_k = jnp.where(ids[k : k + 1, :] == e_f, hit, 0.0)
                hot_st[i * cap : (i + 1) * cap, k * tok : (k + 1) * tok] = hit_k.astype(jnp.bfloat16)
                prob = prob + jnp.sum(hit_k * probs[k : k + 1, :], axis=1, keepdims=True)
            used = jnp.sum(hit, axis=1, keepdims=True)
            index = jnp.sum(hit * lane_f, axis=1, keepdims=True) + 255.0 * (1.0 - used)
            hi = prob.astype(jnp.bfloat16).astype(jnp.float32)
            mid = (prob - hi).astype(jnp.bfloat16).astype(jnp.float32)
            low = prob - hi - mid
            info = jnp.where(
                lane == 0, index, jnp.where(lane == 1, hi, jnp.where(lane == 2, mid, low))
            )
            slots[e, :, first : first + tok] = info.astype(jnp.bfloat16)
        got = jnp.dot(
            hot_st[...], gate_vm[...].reshape(top_k * tok, gate_vm.shape[2]), preferred_element_type=jnp.float32
        ).astype(jnp.bfloat16)
        for i in range(gang):
            e = (me + g * gang + i) % n
            slots[e, :, 0:first] = got[i * cap : (i + 1) * cap, :first]
            late[e] = got[i * cap : (i + 1) * cap, first:]

    late_copy = pltpu.make_async_copy(late, late_out, late_sem)
    late_copy.start()
    landed[me] = slots[me]
    events = [(3, 0), (1, 0), (0, 3), (0, 1), (2, 0), (0, 2)]
    events += [(da, db) for da in (3, 1, 2) for db in (3, 1, 2)]
    to_send = [(0, 0, 1)] + [(4 - da, 4 - db, flip) for da, db in events for flip in range(2)]

    def gate_sends(count):
        for da, db, flip in to_send[:count]:
            e = place(da, db, core) + flip * (1 - 2 * core)
            pltpu.make_async_remote_copy(
                src_ref=slots.at[e],
                dst_ref=landed.at[me],
                send_sem=gate_send.at[e],
                recv_sem=gate_recv.at[me],
                device_id={"expert": e},
                device_id_type=pl.DeviceIdType.MESH,
            ).start()
        del to_send[:count]

    gate_sends(early_gates)

    def gate_copy(peer):
        return pltpu.make_async_remote_copy(
            src_ref=slots.at[peer],
            dst_ref=landed.at[peer],
            send_sem=gate_send.at[peer],
            recv_sem=gate_recv.at[peer],
            device_id={"expert": peer},
            device_id_type=pl.DeviceIdType.MESH,
        )

    outs = []

    def pick(chunk):
        info = landed[chunk, :, first : first + tok].astype(jnp.float32)
        hot = jnp.where(lane_f == info[:, 0:1], 1.0, 0.0).astype(jnp.bfloat16)
        prob = info[:, 1:2] + info[:, 2:3] + info[:, 3:4]
        rows_st[chunk] = jnp.dot(
            hot, held[chunk, 0:tok, :], preferred_element_type=jnp.float32
        ).astype(jnp.bfloat16)
        routed_st[chunk] = (
            prob * jnp.dot(hot, held[chunk, tok : 2 * tok, :], preferred_element_type=jnp.float32)
        ).astype(jnp.bfloat16)
        number = len(outs)
        copies = (
            pltpu.make_async_copy(rows_st.at[chunk], rows_out.at[chunk], out_sem.at[number]),
            pltpu.make_async_copy(routed_st.at[chunk], routed_out.at[chunk], out_sem.at[n + number]),
            pltpu.make_async_copy(
                landed.at[chunk, :, pl.ds(0, first)], gate_out.at[chunk], out_sem.at[2 * n + number]
            ),
        )
        for copy in copies:
            copy.start()
        outs.append(copies)

    def from_sibling(da, db):
        chunk = place(da, db, 1 - core)
        gate_copy(chunk).wait_recv()
        for number in range(pieces):
            arrive(chunk, number)
        pick(chunk)

    pick(me)
    behind = [(0, 0)]
    for da, db in events:
        chunk = place(da, db, core)
        low, high = range(pieces // 2), range(pieces // 2, pieces)
        side = da if db == 0 else db
        for number in (*high, *low) if side == 1 else (*low, *high):
            arrive(chunk, number)
            up, down = (a_up, a_down) if db == 0 else (b_up, b_down)
            if side == 3 and number in low:
                send(chunk, number, up)
            if side == 1 and number in high:
                send(chunk, number, down)
            if db == 0:
                send(chunk, number, b_up)
                send(chunk, number, b_down)
            send(chunk, number, sib)
        gate_sends(2)
        gate_copy(chunk).wait_recv()
        pick(chunk)
        from_sibling(*behind.pop())
        behind.append((da, db))
    from_sibling(*behind.pop())

    for copy in sent:
        copy.wait_send()

    @pl.loop(1, n)
    def _(d):
        gate_copy((me + d) % n).wait_send()

    late_copy.wait()
    for copies in outs:
        for copy in copies:
            copy.wait()


def dispatch(meta, tokens, out_grad, gate_by_k):
    n = lax.axis_size("expert")
    tok, width = tokens.shape
    top_k, _, hidden = gate_by_k.shape
    first = gate_cuts[1]
    bf16 = jnp.bfloat16
    anywhere = pl.BlockSpec(memory_space=pl.ANY)
    return pl.pallas_call(
        functools.partial(dispatch_kernel, first),
        out_shape=(
            jax.ShapeDtypeStruct((n, slot_cap, width), bf16),
            jax.ShapeDtypeStruct((n, slot_cap, width), bf16),
            jax.ShapeDtypeStruct((n, slot_cap, first), bf16),
            jax.ShapeDtypeStruct((n, slot_cap, hidden - first), bf16),
        ),
        in_specs=[pl.BlockSpec(memory_space=pltpu.VMEM), anywhere, anywhere, anywhere],
        out_specs=(anywhere,) * 4,
        scratch_shapes=[
            pltpu.VMEM((n, 2 * tok, width), bf16),
            pltpu.VMEM((n, slot_cap, width), bf16),
            pltpu.VMEM((n, slot_cap, width), bf16),
            pltpu.VMEM((top_k, tok, hidden), bf16),
            pltpu.VMEM((n, slot_cap, first + tok), bf16),
            pltpu.VMEM((n, slot_cap, hidden - first), bf16),
            pltpu.VMEM((n, slot_cap, first + tok), bf16),
            pltpu.VMEM((n, tok), jnp.float32),
            pltpu.VMEM((4 * slot_cap, top_k * tok), bf16),
            pltpu.SemaphoreType.DMA((3,)),
            pltpu.SemaphoreType.DMA((31 * pieces,)),
            pltpu.SemaphoreType.DMA((n, pieces)),
            pltpu.SemaphoreType.DMA((n,)),
            pltpu.SemaphoreType.DMA((n,)),
            pltpu.SemaphoreType.DMA,
            pltpu.SemaphoreType.DMA((3 * n,)),
        ],
        compiler_params=pltpu.CompilerParams(
            collective_id=0, has_side_effects=True, vmem_limit_bytes=62 << 20
        ),
        cost_estimate=pl.CostEstimate(
            flops=8 * n * slot_cap * tok * width, bytes_accessed=100 << 20, transcendentals=0
        ),
    )(meta, tokens, out_grad, gate_by_k)


def reduce_kernel(
    cuts,
    rows_ref,
    routed_ref,
    gate_1st,
    up_1st,
    gate_ref,
    up_ref,
    hidden_1st,
    hidden_2nd,
    gate_mat,
    up_mat,
    gate_out,
    up_out,
    down_out,
    returned,
    hidden_ref,
    back,
    mats,
    wide,
    tall,
    wide_first,
    tall_first,
    wide_send,
    wide_recv,
    tall_send,
    tall_recv,
    mat_sem,
    back_send,
    back_recv,
    own_sem,
):
    n = hidden_ref.shape[0]
    n_peers, cap = back.shape[:2]
    here = lax.axis_index("expert")
    first = cuts[1]
    me = lax.axis_index("dp")
    quarter = gate_out.shape[0]
    half = tall_first.shape[2]
    ahead, behind = (me + 1) % n, (me + n - 1) % n

    barrier = pltpu.get_barrier_semaphore()
    for to in (ahead, behind):
        pl.semaphore_signal(
            barrier, inc=1, device_id={"dp": to}, device_id_type=pl.DeviceIdType.MESH
        )

    @pl.loop(1, n_peers)
    def _(d):
        pl.semaphore_signal(
            barrier,
            inc=1,
            device_id={"expert": (here + d) % n_peers},
            device_id_type=pl.DeviceIdType.MESH,
        )

    pl.semaphore_wait(barrier, n_peers + 1)

    tile = mats.shape[2]
    n_tiles = gate_mat.shape[0] // tile

    def mat_loads(t):
        return [
            pltpu.make_async_copy(
                mat.at[pl.ds(t * tile, tile)], mats.at[t % 2, i], mat_sem.at[t % 2, i]
            )
            for i, mat in enumerate((gate_mat, up_mat))
        ]

    for t in range(2):
        for load in mat_loads(t):
            load.start()

    def copy_of(which, way, hop):
        first, landed, send_sem, recv_sem = (
            (wide_first, wide, wide_send, wide_recv) if which == 0 else (tall_first, tall, tall_send, tall_recv)
        )
        return pltpu.make_async_remote_copy(
            src_ref=first.at[way] if hop == 0 else landed.at[way, hop - 1],
            dst_ref=landed.at[way, hop],
            send_sem=send_sem.at[way, hop],
            recv_sem=recv_sem.at[way, hop],
            device_id={"dp": ahead if way == 0 else behind},
            device_id_type=pl.DeviceIdType.MESH,
        )

    def term(which, way, share):
        if which == 0:
            columns = pl.ds(pl.multiple_of(share * quarter, quarter), quarter)
            got = mm(rows_ref[:, columns], (gate_ref if way == 0 else up_ref)[...], 0, 0)
        else:
            got = mm(hidden_ref[share], routed_ref[:, way * half : (way + 1) * half], 0, 0)
        return grad_scale * got

    def step(hop, which):
        for way in range(2):
            share = (me + n - 1 - hop) % n if way == 0 else (me + 1 + hop) % n
            part = term(which, way, share)
            if hop == 0:
                start = wide_first if which == 0 else tall_first
                start[way] = part.astype(jnp.bfloat16)
            else:
                landed = wide if which == 0 else tall
                copy_of(which, way, hop - 1).wait_recv()
                part = (part + landed[way, hop - 1].astype(jnp.float32)).astype(jnp.bfloat16)
                if hop < n - 1:
                    landed[way, hop - 1] = part
                elif which == 0:
                    (gate_out if way == 0 else up_out)[...] = part
                else:
                    down_out[:, way * half : (way + 1) * half] = part
            if hop < n - 1:
                copy_of(which, way, hop).start()

    step(0, 0)

    tall_rows = hidden_ref.shape[2]
    row_block = 256

    @pl.loop(0, hidden_ref.shape[1] // row_block)
    def _(r):
        rows = pl.ds(pl.multiple_of(r * row_block, row_block), row_block)
        for q in range(n):
            for source, a, b in ((hidden_1st, 0, first), (hidden_2nd, first, cuts[2])):
                low, high = max(a, q * tall_rows), min(b, (q + 1) * tall_rows)
                if low < high:
                    hidden_ref[q, rows, low - q * tall_rows : high - q * tall_rows] = source[
                        rows, low - a : high - a
                    ]

    step(0, 1)

    gang = 8
    n_gangs = n_peers // gang
    per_send = n_tiles // 2
    send_cols = per_send * tile

    def back_copy(part, peer, at):
        columns = pl.ds(part * send_cols, send_cols)
        return pltpu.make_async_remote_copy(
            src_ref=back.at[peer, :, columns],
            dst_ref=returned.at[at, :, columns],
            send_sem=back_send.at[part, peer],
            recv_sem=back_recv.at[part, at],
            device_id={"expert": peer},
            device_id_type=pl.DeviceIdType.MESH,
        )

    for t in range(n_tiles):
        for load in mat_loads(t):
            load.wait()

        @pl.loop(0, n_gangs)
        def _(m):
            rows = pl.ds(pl.multiple_of(m * gang * cap, gang * cap), gang * cap)
            total = mm(gate_1st[rows, :], mats[t % 2, 0, :, :first], 1, 1)
            total = total + mm(gate_ref[rows, :], mats[t % 2, 0, :, first:], 1, 1)
            total = total + mm(up_1st[rows, :], mats[t % 2, 1, :, :first], 1, 1)
            total = total + mm(up_ref[rows, :], mats[t % 2, 1, :, first:], 1, 1)
            back[pl.ds(m * gang, gang), :, t * tile : (t + 1) * tile] = total.astype(
                jnp.bfloat16
            ).reshape(gang, cap, tile)

        if t + 2 < n_tiles:
            for load in mat_loads(t + 2):
                load.start()
        if (t + 1) % per_send == 0:

            @pl.loop(1, n_peers)
            def _(d):
                back_copy(t // per_send, (here + d) % n_peers, here).start()

    own = pltpu.make_async_copy(back.at[here], returned.at[here], own_sem)
    own.start()

    for hop in range(1, n):
        for which in range(2):
            step(hop, which)

    for hop in range(n - 1):
        for which in range(2):
            for way in range(2):
                copy_of(which, way, hop).wait_send()
    own.wait()
    for part in range(2):

        @pl.loop(1, n_peers)
        def _(d):
            peer = (here + d) % n_peers
            back_copy(part, peer, peer).wait_recv()
            back_copy(part, peer, peer).wait_send()


def reduce_late(rows_in, routed, grads, hidden, gate_mat, up_mat):
    n = lax.axis_size("dp")
    n_peers = lax.axis_size("expert")
    slots, width = rows_in.shape
    cols = gate_cuts[2] - gate_cuts[1]
    tall_rows = gate_cuts[2] // n
    quarter, half, tile = width // n, width // 2, width // 4
    bf16 = jnp.bfloat16
    vmem = pl.BlockSpec(memory_space=pltpu.VMEM)
    anywhere = pl.BlockSpec(memory_space=pl.ANY)
    return pl.pallas_call(
        functools.partial(reduce_kernel, gate_cuts),
        out_shape=(
            jax.ShapeDtypeStruct((quarter, cols), bf16),
            jax.ShapeDtypeStruct((quarter, cols), bf16),
            jax.ShapeDtypeStruct((tall_rows, width), bf16),
            jax.ShapeDtypeStruct((n_peers, slot_cap, width), bf16),
        ),
        in_specs=[vmem] * 8 + [anywhere] * 2,
        out_specs=(vmem, vmem, vmem, anywhere),
        scratch_shapes=[
            pltpu.VMEM((n, slots, tall_rows), bf16),
            pltpu.VMEM((n_peers, slot_cap, width), bf16),
            pltpu.VMEM((2, 2, tile, gate_cuts[2]), bf16),
            pltpu.VMEM((2, n - 1, quarter, cols), bf16),
            pltpu.VMEM((2, n - 1, tall_rows, half), bf16),
            pltpu.VMEM((2, quarter, cols), bf16),
            pltpu.VMEM((2, tall_rows, half), bf16),
            pltpu.SemaphoreType.DMA((2, n - 1)),
            pltpu.SemaphoreType.DMA((2, n - 1)),
            pltpu.SemaphoreType.DMA((2, n - 1)),
            pltpu.SemaphoreType.DMA((2, n - 1)),
            pltpu.SemaphoreType.DMA((2, 2)),
            pltpu.SemaphoreType.DMA((2, n_peers)),
            pltpu.SemaphoreType.DMA((2, n_peers)),
            pltpu.SemaphoreType.DMA,
        ],
        compiler_params=pltpu.CompilerParams(
            collective_id=1, has_side_effects=True, vmem_limit_bytes=63 << 20
        ),
        cost_estimate=pl.CostEstimate(
            flops=2 * slots * width * (4 * cols + 3 * n * tall_rows),
            bytes_accessed=300 << 20,
            transcendentals=0,
        ),
    )(rows_in, routed, *grads, *hidden, gate_mat, up_mat)


def local(tokens, out_grad, gate_saved, probs, expert_ids, w_gate, w_up, w_down):
    n_peers = lax.axis_size("expert")
    tok_rows, model_width = tokens.shape
    top_k = expert_ids.shape[1]
    n_slots = n_peers * slot_cap
    gate_mat, up_mat, down_mat = w_gate[0], w_up[0], w_down[0]

    ids_t = expert_ids.T
    meta = jnp.concatenate(
        [ids_t.astype(jnp.float32), probs.T, jnp.zeros((16 - 2 * top_k, tok_rows), jnp.float32)], axis=0
    )
    rows_in, routed, gate_first, gate_late = dispatch(
        meta, tokens, out_grad, jnp.transpose(gate_saved, (1, 0, 2))
    )
    rows_in = rows_in.reshape(n_slots, model_width)
    routed = routed.reshape(n_slots, model_width)
    gate_late = lax.all_to_all(gate_late, "expert", split_axis=0, concat_axis=0, tiled=True)
    recv_gate = [g.reshape(n_slots, g.shape[2]) for g in (gate_first, gate_late)]

    experts = lax.broadcasted_iota(jnp.int32, (n_peers, 1, 1), 0)
    chosen = jnp.any(ids_t[None] == experts, axis=1)
    before = (
        lax.broadcasted_iota(jnp.int32, (tok_rows, tok_rows), 0)
        < lax.broadcasted_iota(jnp.int32, (tok_rows, tok_rows), 1)
    ).astype(jnp.bfloat16)
    rank = mm(chosen.astype(jnp.bfloat16), before, 1, 0).astype(jnp.int32)
    slots = lax.broadcasted_iota(jnp.int32, (1, slot_cap, 1), 1)
    send_hot = (rank[:, None, :] == slots) & chosen[:, None, :]

    hidden, gate_grads, up_grads, first_share = [], [], [], None
    for j, (a, b) in enumerate(zip(gate_cuts, gate_cuts[1:])):
        hidden_grad = mm(routed, down_mat[a:b, :], 1, 1)
        up_act = mm(rows_in, up_mat[:, a:b], 1, 0)
        gate_val = recv_gate[j].astype(jnp.float32)
        gate_sig = jax.nn.sigmoid(gate_val)
        gate_act = gate_val * gate_sig
        hidden.append((gate_act * up_act).astype(jnp.bfloat16))
        up_grad = (hidden_grad * gate_act).astype(jnp.bfloat16)
        gate_grad = (hidden_grad * up_act * gate_sig * (1.0 + gate_val * (1.0 - gate_sig))).astype(
            jnp.bfloat16
        )
        gate_grads.append(gate_grad)
        up_grads.append(up_grad)
        if j == 0:
            both = jnp.concatenate([gate_grad, up_grad], axis=1)
            term = (grad_scale * mm(rows_in, both, 0, 0)).astype(jnp.bfloat16)
            first_share = lax.psum_scatter(term, "dp", scatter_dimension=0, tiled=True)

    grads = (gate_grads[0], up_grads[0], gate_grads[1], up_grads[1])
    late_gate, late_up, grad_down, returned = reduce_late(
        rows_in, routed, grads, hidden, gate_mat, up_mat
    )
    input_grad = mm(
        send_hot.reshape(n_slots, tok_rows).astype(jnp.bfloat16),
        returned.reshape(n_slots, model_width),
        0,
        0,
    ).astype(jnp.bfloat16)

    first = gate_cuts[1]
    grad_gate = jnp.concatenate([first_share[:, :first], late_gate], axis=1)
    grad_up = jnp.concatenate([first_share[:, first:], late_up], axis=1)
    return (input_grad, grad_gate[None], grad_up[None], grad_down[None])


def solution(mesh):
    return jax.shard_map(
        local,
        mesh=mesh,
        in_specs=(
            P(("dp", "expert"), None),
            P(("dp", "expert"), None),
            P(("dp", "expert"), None, None),
            P(("dp", "expert"), None),
            P(("dp", "expert"), None),
            P("expert", None, None),
            P("expert", None, None),
            P("expert", None, None),
        ),
        out_specs=(
            P(("dp", "expert"), None),
            P("expert", "dp", None),
            P("expert", "dp", None),
            P("expert", "dp", None),
        ),
        check_vma=False,
    )
```

```python
import functools

import jax
import jax.numpy as jnp
from jax import lax
from jax.experimental import pallas as pl
from jax.experimental.pallas import tpu as pltpu
from jax.sharding import PartitionSpec as P

grad_scale = 0.0625
slot_cap = 48
gate_cuts = (0, 768, 1408)
pieces = 2
early_gates = 9


def mm(a, b, ca, cb):
    return lax.dot_general(a, b, (((ca,), (cb,)), ((), ())), preferred_element_type=jnp.float32)


def dispatch_kernel(
    first,
    meta_ref,
    tok_hbm,
    grad_hbm,
    gate_hbm,
    rows_out,
    routed_out,
    gate_out,
    late_out,
    held,
    rows_st,
    routed_st,
    gate_vm,
    slots,
    late,
    landed,
    slot_of,
    hot_st,
    load_sem,
    send_sem,
    recv_sem,
    gate_send,
    gate_recv,
    late_sem,
    out_sem,
):
    n = slots.shape[0]
    tok = tok_hbm.shape[0]
    cap = slots.shape[1]
    top_k = gate_hbm.shape[0]
    me = lax.axis_index("expert")
    core = me % 2
    x = (me // 2) % 4
    y = me // 8
    sib = me + 1 - 2 * core

    def place(da, db, c):
        dx = da * (1 - c) + db * c
        dy = da * c + db * (1 - c)
        return (((y + dy) % 4) * 4 + (x + dx) % 4) * 2 + c

    loads = [
        pltpu.make_async_copy(tok_hbm, held.at[me, pl.ds(0, tok)], load_sem.at[0]),
        pltpu.make_async_copy(grad_hbm, held.at[me, pl.ds(tok, tok)], load_sem.at[1]),
        pltpu.make_async_copy(gate_hbm, gate_vm, load_sem.at[2]),
    ]
    for load in loads:
        load.start()

    barrier = pltpu.get_barrier_semaphore()

    @pl.loop(1, n)
    def _(d):
        pl.semaphore_signal(
            barrier, inc=1, device_id={"expert": (me + d) % n}, device_id_type=pl.DeviceIdType.MESH
        )

    pl.semaphore_wait(barrier, n - 1)

    sent = []

    piece = held.shape[1] // pieces

    def send(chunk, number, to):
        part = held.at[chunk, pl.ds(number * piece, piece)]
        copy = pltpu.make_async_remote_copy(
            src_ref=part,
            dst_ref=part,
            send_sem=send_sem.at[len(sent)],
            recv_sem=recv_sem.at[chunk, number],
            device_id={"expert": to},
            device_id_type=pl.DeviceIdType.MESH,
        )
        copy.start()
        sent.append(copy)

    def arrive(chunk, number):
        part = held.at[chunk, pl.ds(number * piece, piece)]
        pltpu.make_async_remote_copy(
            src_ref=part,
            dst_ref=part,
            send_sem=send_sem.at[0],
            recv_sem=recv_sem.at[chunk, number],
            device_id={"expert": sib},
            device_id_type=pl.DeviceIdType.MESH,
        ).wait_recv()

    a_up, a_down = place(1, 0, core), place(3, 0, core)
    b_up, b_down = place(0, 1, core), place(0, 3, core)

    for number in range(pieces):
        if number % (pieces // 2) == 0:
            loads[number // (pieces // 2)].wait()
        for to in (a_up, a_down, b_up, b_down, sib):
            send(me, number, to)

    ids = meta_ref[0:top_k, :]
    probs = meta_ref[top_k : 2 * top_k, :]
    peers = lax.broadcasted_iota(jnp.int32, (n, tok), 0).astype(jnp.float32)
    chosen = jnp.zeros((n, tok), jnp.float32)
    for k in range(top_k):
        chosen = jnp.where(peers == ids[k : k + 1, :], 1.0, chosen)
    before = (
        lax.broadcasted_iota(jnp.int32, (tok, tok), 0) < lax.broadcasted_iota(jnp.int32, (tok, tok), 1)
    ).astype(jnp.float32)
    rank = jnp.dot(
        chosen.astype(jnp.bfloat16), before.astype(jnp.bfloat16), preferred_element_type=jnp.float32
    )
    slot_of[...] = jnp.where(chosen > 0.0, rank, -1.0)
    loads[2].wait()

    lane = lax.broadcasted_iota(jnp.int32, (cap, tok), 1)
    lane_f = lane.astype(jnp.float32)
    slot_f = lax.broadcasted_iota(jnp.int32, (cap, tok), 0).astype(jnp.float32)
    gang = hot_st.shape[0] // cap

    @pl.loop(0, n // gang)
    def _(g):
        for i in range(gang):
            e = (me + g * gang + i) % n
            e_f = e.astype(jnp.float32)
            hit = jnp.where(slot_f == slot_of[pl.ds(e, 1), :], 1.0, 0.0)
            prob = jnp.zeros((cap, 1), jnp.float32)
            for k in range(top_k):
                hit_k = jnp.where(ids[k : k + 1, :] == e_f, hit, 0.0)
                hot_st[i * cap : (i + 1) * cap, k * tok : (k + 1) * tok] = hit_k.astype(jnp.bfloat16)
                prob = prob + jnp.sum(hit_k * probs[k : k + 1, :], axis=1, keepdims=True)
            used = jnp.sum(hit, axis=1, keepdims=True)
            index = jnp.sum(hit * lane_f, axis=1, keepdims=True) + 255.0 * (1.0 - used)
            hi = prob.astype(jnp.bfloat16).astype(jnp.float32)
            mid = (prob - hi).astype(jnp.bfloat16).astype(jnp.float32)
            low = prob - hi - mid
            info = jnp.where(
                lane == 0, index, jnp.where(lane == 1, hi, jnp.where(lane == 2, mid, low))
            )
            slots[e, :, first : first + tok] = info.astype(jnp.bfloat16)
        got = jnp.dot(
            hot_st[...], gate_vm[...].reshape(top_k * tok, gate_vm.shape[2]), preferred_element_type=jnp.float32
        ).astype(jnp.bfloat16)
        for i in range(gang):
            e = (me + g * gang + i) % n
            slots[e, :, 0:first] = got[i * cap : (i + 1) * cap, :first]
            late[e] = got[i * cap : (i + 1) * cap, first:]

    late_copy = pltpu.make_async_copy(late, late_out, late_sem)
    late_copy.start()
    landed[me] = slots[me]
    events = [(3, 0), (1, 0), (0, 3), (0, 1), (2, 0), (0, 2)]
    events += [(da, db) for da in (3, 1, 2) for db in (3, 1, 2)]
    to_send = [(0, 0, 1)] + [(4 - da, 4 - db, flip) for da, db in events for flip in range(2)]

    def gate_sends(count):
        for da, db, flip in to_send[:count]:
            e = place(da, db, core) + flip * (1 - 2 * core)
            pltpu.make_async_remote_copy(
                src_ref=slots.at[e],
                dst_ref=landed.at[me],
                send_sem=gate_send.at[e],
                recv_sem=gate_recv.at[me],
                device_id={"expert": e},
                device_id_type=pl.DeviceIdType.MESH,
            ).start()
        del to_send[:count]

    gate_sends(early_gates)

    def gate_copy(peer):
        return pltpu.make_async_remote_copy(
            src_ref=slots.at[peer],
            dst_ref=landed.at[peer],
            send_sem=gate_send.at[peer],
            recv_sem=gate_recv.at[peer],
            device_id={"expert": peer},
            device_id_type=pl.DeviceIdType.MESH,
        )

    outs = []

    def pick(chunk):
        info = landed[chunk, :, first : first + tok].astype(jnp.float32)
        hot = jnp.where(lane_f == info[:, 0:1], 1.0, 0.0).astype(jnp.bfloat16)
        prob = info[:, 1:2] + info[:, 2:3] + info[:, 3:4]
        rows_st[chunk] = jnp.dot(
            hot, held[chunk, 0:tok, :], preferred_element_type=jnp.float32
        ).astype(jnp.bfloat16)
        routed_st[chunk] = (
            prob * jnp.dot(hot, held[chunk, tok : 2 * tok, :], preferred_element_type=jnp.float32)
        ).astype(jnp.bfloat16)
        number = len(outs)
        copies = (
            pltpu.make_async_copy(rows_st.at[chunk], rows_out.at[chunk], out_sem.at[number]),
            pltpu.make_async_copy(routed_st.at[chunk], routed_out.at[chunk], out_sem.at[n + number]),
            pltpu.make_async_copy(
                landed.at[chunk, :, pl.ds(0, first)], gate_out.at[chunk], out_sem.at[2 * n + number]
            ),
        )
        for copy in copies:
            copy.start()
        outs.append(copies)

    def from_sibling(da, db):
        chunk = place(da, db, 1 - core)
        gate_copy(chunk).wait_recv()
        for number in range(pieces):
            arrive(chunk, number)
        pick(chunk)

    pick(me)
    behind = [(0, 0)]
    for da, db in events:
        chunk = place(da, db, core)
        low, high = range(pieces // 2), range(pieces // 2, pieces)
        side = da if db == 0 else db
        for number in (*high, *low) if side == 1 else (*low, *high):
            arrive(chunk, number)
            up, down = (a_up, a_down) if db == 0 else (b_up, b_down)
            if side == 3 and number in low:
                send(chunk, number, up)
            if side == 1 and number in high:
                send(chunk, number, down)
            if db == 0:
                send(chunk, number, b_up)
                send(chunk, number, b_down)
            send(chunk, number, sib)
        gate_sends(2)
        gate_copy(chunk).wait_recv()
        pick(chunk)
        from_sibling(*behind.pop())
        behind.append((da, db))
    from_sibling(*behind.pop())

    for copy in sent:
        copy.wait_send()

    @pl.loop(1, n)
    def _(d):
        gate_copy((me + d) % n).wait_send()

    late_copy.wait()
    for copies in outs:
        for copy in copies:
            copy.wait()


def dispatch(meta, tokens, out_grad, gate_by_k):
    n = lax.axis_size("expert")
    tok, width = tokens.shape
    top_k, _, hidden = gate_by_k.shape
    first = gate_cuts[1]
    bf16 = jnp.bfloat16
    anywhere = pl.BlockSpec(memory_space=pl.ANY)
    return pl.pallas_call(
        functools.partial(dispatch_kernel, first),
        out_shape=(
            jax.ShapeDtypeStruct((n, slot_cap, width), bf16),
            jax.ShapeDtypeStruct((n, slot_cap, width), bf16),
            jax.ShapeDtypeStruct((n, slot_cap, first), bf16),
            jax.ShapeDtypeStruct((n, slot_cap, hidden - first), bf16),
        ),
        in_specs=[pl.BlockSpec(memory_space=pltpu.VMEM), anywhere, anywhere, anywhere],
        out_specs=(anywhere,) * 4,
        scratch_shapes=[
            pltpu.VMEM((n, 2 * tok, width), bf16),
            pltpu.VMEM((n, slot_cap, width), bf16),
            pltpu.VMEM((n, slot_cap, width), bf16),
            pltpu.VMEM((top_k, tok, hidden), bf16),
            pltpu.VMEM((n, slot_cap, first + tok), bf16),
            pltpu.VMEM((n, slot_cap, hidden - first), bf16),
            pltpu.VMEM((n, slot_cap, first + tok), bf16),
            pltpu.VMEM((n, tok), jnp.float32),
            pltpu.VMEM((4 * slot_cap, top_k * tok), bf16),
            pltpu.SemaphoreType.DMA((3,)),
            pltpu.SemaphoreType.DMA((31 * pieces,)),
            pltpu.SemaphoreType.DMA((n, pieces)),
            pltpu.SemaphoreType.DMA((n,)),
            pltpu.SemaphoreType.DMA((n,)),
            pltpu.SemaphoreType.DMA,
            pltpu.SemaphoreType.DMA((3 * n,)),
        ],
        compiler_params=pltpu.CompilerParams(
            collective_id=0, has_side_effects=True, vmem_limit_bytes=62 << 20
        ),
        cost_estimate=pl.CostEstimate(
            flops=8 * n * slot_cap * tok * width, bytes_accessed=100 << 20, transcendentals=0
        ),
    )(meta, tokens, out_grad, gate_by_k)


def reduce_kernel(
    cuts,
    *refs,
):
    sources, refs = refs[:8], refs[8:]
    loaded, refs = refs[6 : 6 + 8], refs[:6] + refs[6 + 8 :]
    reduce_body(cuts, sources, loaded, *refs)


def reduce_body(
    cuts,
    sources,
    loaded,
    gate_mat,
    up_mat,
    gate_out,
    up_out,
    down_out,
    returned,
    hidden_ref,
    back,
    mats,
    wide,
    tall,
    wide_first,
    tall_first,
    wide_send,
    wide_recv,
    tall_send,
    tall_recv,
    mat_sem,
    back_send,
    back_recv,
    own_sem,
    load_sem,
):
    gate_1st, up_1st, gate_ref, up_ref, rows_ref, hidden_1st, hidden_2nd, routed_ref = loaded
    loads = [
        pltpu.make_async_copy(source, loaded[i], load_sem.at[i]) for i, source in enumerate(sources)
    ]
    n = hidden_ref.shape[0]
    n_peers, cap = back.shape[:2]
    here = lax.axis_index("expert")
    first = cuts[1]
    me = lax.axis_index("dp")
    quarter = gate_out.shape[0]
    half = tall_first.shape[2]
    ahead, behind = (me + 1) % n, (me + n - 1) % n

    tile = mats.shape[2]
    n_tiles = gate_mat.shape[0] // tile

    def mat_loads(t):
        return [
            pltpu.make_async_copy(
                mat.at[pl.ds(t * tile, tile)], mats.at[t % 2, i], mat_sem.at[t % 2, i]
            )
            for i, mat in enumerate((gate_mat, up_mat))
        ]

    for t in range(2):
        for load in mat_loads(t):
            load.start()
    for load in loads:
        load.start()

    barrier = pltpu.get_barrier_semaphore()
    for to in (ahead, behind):
        pl.semaphore_signal(
            barrier, inc=1, device_id={"dp": to}, device_id_type=pl.DeviceIdType.MESH
        )

    @pl.loop(1, n_peers)
    def _(d):
        pl.semaphore_signal(
            barrier,
            inc=1,
            device_id={"expert": (here + d) % n_peers},
            device_id_type=pl.DeviceIdType.MESH,
        )

    pl.semaphore_wait(barrier, n_peers + 1)

    def copy_of(which, way, hop):
        first, landed, send_sem, recv_sem = (
            (wide_first, wide, wide_send, wide_recv) if which == 0 else (tall_first, tall, tall_send, tall_recv)
        )
        return pltpu.make_async_remote_copy(
            src_ref=first.at[way] if hop == 0 else landed.at[way, hop - 1],
            dst_ref=landed.at[way, hop],
            send_sem=send_sem.at[way, hop],
            recv_sem=recv_sem.at[way, hop],
            device_id={"dp": ahead if way == 0 else behind},
            device_id_type=pl.DeviceIdType.MESH,
        )

    def term(which, way, share):
        if which == 0:
            columns = pl.ds(pl.multiple_of(share * quarter, quarter), quarter)
            got = mm(rows_ref[:, columns], (gate_ref if way == 0 else up_ref)[...], 0, 0)
        else:
            got = mm(hidden_ref[share], routed_ref[:, way * half : (way + 1) * half], 0, 0)
        return grad_scale * got

    def step(hop, which):
        for way in range(2):
            share = (me + n - 1 - hop) % n if way == 0 else (me + 1 + hop) % n
            part = term(which, way, share)
            if hop == 0:
                start = wide_first if which == 0 else tall_first
                start[way] = part.astype(jnp.bfloat16)
            else:
                landed = wide if which == 0 else tall
                copy_of(which, way, hop - 1).wait_recv()
                part = (part + landed[way, hop - 1].astype(jnp.float32)).astype(jnp.bfloat16)
                if hop < n - 1:
                    landed[way, hop - 1] = part
                elif which == 0:
                    (gate_out if way == 0 else up_out)[...] = part
                else:
                    down_out[:, way * half : (way + 1) * half] = part
            if hop < n - 1:
                copy_of(which, way, hop).start()

    def split_hidden():
        tall_rows = hidden_ref.shape[2]
        row_block = 256

        @pl.loop(0, hidden_ref.shape[1] // row_block)
        def _(r):
            rows = pl.ds(pl.multiple_of(r * row_block, row_block), row_block)
            for q in range(n):
                for source, a, b in ((hidden_1st, 0, first), (hidden_2nd, first, cuts[2])):
                    low, high = max(a, q * tall_rows), min(b, (q + 1) * tall_rows)
                    if low < high:
                        hidden_ref[q, rows, low - q * tall_rows : high - q * tall_rows] = source[
                            rows, low - a : high - a
                        ]

    gang = 8
    n_gangs = n_peers // gang

    def back_copy(part, peer, at):
        columns = pl.ds(part * tile, tile)
        return pltpu.make_async_remote_copy(
            src_ref=back.at[peer, :, columns],
            dst_ref=returned.at[at, :, columns],
            send_sem=back_send.at[part, peer],
            recv_sem=back_recv.at[part, at],
            device_id={"expert": peer},
            device_id_type=pl.DeviceIdType.MESH,
        )

    def input_tile(t):
        for load in mat_loads(t):
            load.wait()

        @pl.loop(0, n_gangs)
        def _(m):
            rows = pl.ds(pl.multiple_of(m * gang * cap, gang * cap), gang * cap)
            total = mm(gate_1st[rows, :], mats[t % 2, 0, :, :first], 1, 1)
            total = total + mm(gate_ref[rows, :], mats[t % 2, 0, :, first:], 1, 1)
            total = total + mm(up_1st[rows, :], mats[t % 2, 1, :, :first], 1, 1)
            total = total + mm(up_ref[rows, :], mats[t % 2, 1, :, first:], 1, 1)
            back[pl.ds(m * gang, gang), :, t * tile : (t + 1) * tile] = total.astype(
                jnp.bfloat16
            ).reshape(gang, cap, tile)

        if t + 2 < n_tiles:
            for load in mat_loads(t + 2):
                load.start()
        @pl.loop(1, n_peers)
        def _(d):
            back_copy(t, (here + d) % n_peers, here).start()

    for load in loads[:4]:
        load.wait()
    loads[4].wait()
    step(0, 0)
    input_tile(0)
    input_tile(1)
    for load in loads[5:]:
        load.wait()
    split_hidden()
    step(0, 1)
    input_tile(2)
    input_tile(3)

    own = pltpu.make_async_copy(back.at[here], returned.at[here], own_sem)
    own.start()

    for hop in range(1, n):
        for which in range(2):
            step(hop, which)

    for hop in range(n - 1):
        for which in range(2):
            for way in range(2):
                copy_of(which, way, hop).wait_send()
    own.wait()
    for part in range(n_tiles):

        @pl.loop(1, n_peers)
        def _(d):
            peer = (here + d) % n_peers
            back_copy(part, peer, peer).wait_recv()
            back_copy(part, peer, peer).wait_send()


def reduce_late(rows_in, routed, grads, hidden, gate_mat, up_mat):
    n = lax.axis_size("dp")
    n_peers = lax.axis_size("expert")
    slots, width = rows_in.shape
    cols = gate_cuts[2] - gate_cuts[1]
    tall_rows = gate_cuts[2] // n
    quarter, half, tile = width // n, width // 2, width // 4
    bf16 = jnp.bfloat16
    vmem = pl.BlockSpec(memory_space=pltpu.VMEM)
    anywhere = pl.BlockSpec(memory_space=pl.ANY)
    sources = (*grads, rows_in, *hidden, routed)
    return pl.pallas_call(
        functools.partial(reduce_kernel, gate_cuts),
        out_shape=(
            jax.ShapeDtypeStruct((quarter, cols), bf16),
            jax.ShapeDtypeStruct((quarter, cols), bf16),
            jax.ShapeDtypeStruct((tall_rows, width), bf16),
            jax.ShapeDtypeStruct((n_peers, slot_cap, width), bf16),
        ),
        in_specs=[anywhere] * 10,
        out_specs=(vmem, vmem, vmem, anywhere),
        scratch_shapes=[pltpu.VMEM(source.shape, bf16) for source in sources]
        + [
            pltpu.VMEM((n, slots, tall_rows), bf16),
            pltpu.VMEM((n_peers, slot_cap, width), bf16),
            pltpu.VMEM((2, 2, tile, gate_cuts[2]), bf16),
            pltpu.VMEM((2, n - 1, quarter, cols), bf16),
            pltpu.VMEM((2, n - 1, tall_rows, half), bf16),
            pltpu.VMEM((2, quarter, cols), bf16),
            pltpu.VMEM((2, tall_rows, half), bf16),
            pltpu.SemaphoreType.DMA((2, n - 1)),
            pltpu.SemaphoreType.DMA((2, n - 1)),
            pltpu.SemaphoreType.DMA((2, n - 1)),
            pltpu.SemaphoreType.DMA((2, n - 1)),
            pltpu.SemaphoreType.DMA((2, 2)),
            pltpu.SemaphoreType.DMA((4, n_peers)),
            pltpu.SemaphoreType.DMA((4, n_peers)),
            pltpu.SemaphoreType.DMA,
            pltpu.SemaphoreType.DMA((8,)),
        ],
        compiler_params=pltpu.CompilerParams(
            collective_id=1, has_side_effects=True, vmem_limit_bytes=63 << 20
        ),
        cost_estimate=pl.CostEstimate(
            flops=2 * slots * width * (4 * cols + 3 * n * tall_rows),
            bytes_accessed=300 << 20,
            transcendentals=0,
        ),
    )(*sources, gate_mat, up_mat)


def local(tokens, out_grad, gate_saved, probs, expert_ids, w_gate, w_up, w_down):
    n_peers = lax.axis_size("expert")
    tok_rows, model_width = tokens.shape
    top_k = expert_ids.shape[1]
    n_slots = n_peers * slot_cap
    gate_mat, up_mat, down_mat = w_gate[0], w_up[0], w_down[0]

    ids_t = expert_ids.T
    meta = jnp.concatenate(
        [ids_t.astype(jnp.float32), probs.T, jnp.zeros((16 - 2 * top_k, tok_rows), jnp.float32)], axis=0
    )
    rows_in, routed, gate_first, gate_late = dispatch(
        meta, tokens, out_grad, jnp.transpose(gate_saved, (1, 0, 2))
    )
    rows_in = rows_in.reshape(n_slots, model_width)
    routed = routed.reshape(n_slots, model_width)
    gate_late = lax.all_to_all(gate_late, "expert", split_axis=0, concat_axis=0, tiled=True)
    recv_gate = [g.reshape(n_slots, g.shape[2]) for g in (gate_first, gate_late)]

    experts = lax.broadcasted_iota(jnp.int32, (n_peers, 1, 1), 0)
    chosen = jnp.any(ids_t[None] == experts, axis=1)
    before = (
        lax.broadcasted_iota(jnp.int32, (tok_rows, tok_rows), 0)
        < lax.broadcasted_iota(jnp.int32, (tok_rows, tok_rows), 1)
    ).astype(jnp.bfloat16)
    rank = mm(chosen.astype(jnp.bfloat16), before, 1, 0).astype(jnp.int32)
    slots = lax.broadcasted_iota(jnp.int32, (1, slot_cap, 1), 1)
    send_hot = (rank[:, None, :] == slots) & chosen[:, None, :]

    hidden, gate_grads, up_grads, first_share = [], [], [], None
    for j, (a, b) in enumerate(zip(gate_cuts, gate_cuts[1:])):
        hidden_grad = mm(routed, down_mat[a:b, :], 1, 1)
        up_act = mm(rows_in, up_mat[:, a:b], 1, 0)
        gate_val = recv_gate[j].astype(jnp.float32)
        gate_sig = jax.nn.sigmoid(gate_val)
        gate_act = gate_val * gate_sig
        hidden.append((gate_act * up_act).astype(jnp.bfloat16))
        up_grad = (hidden_grad * gate_act).astype(jnp.bfloat16)
        gate_grad = (hidden_grad * up_act * gate_sig * (1.0 + gate_val * (1.0 - gate_sig))).astype(
            jnp.bfloat16
        )
        gate_grads.append(gate_grad)
        up_grads.append(up_grad)
        if j == 0:
            both = jnp.concatenate([gate_grad, up_grad], axis=1)
            term = (grad_scale * mm(rows_in, both, 0, 0)).astype(jnp.bfloat16)
            first_share = lax.psum_scatter(term, "dp", scatter_dimension=0, tiled=True)

    grads = (gate_grads[0], up_grads[0], gate_grads[1], up_grads[1])
    late_gate, late_up, grad_down, returned = reduce_late(
        rows_in, routed, grads, hidden, gate_mat, up_mat
    )
    input_grad = mm(
        send_hot.reshape(n_slots, tok_rows).astype(jnp.bfloat16),
        returned.reshape(n_slots, model_width),
        0,
        0,
    ).astype(jnp.bfloat16)

    first = gate_cuts[1]
    grad_gate = jnp.concatenate([first_share[:, :first], late_gate], axis=1)
    grad_up = jnp.concatenate([first_share[:, first:], late_up], axis=1)
    return (input_grad, grad_gate[None], grad_up[None], grad_down[None])


def solution(mesh):
    return jax.shard_map(
        local,
        mesh=mesh,
        in_specs=(
            P(("dp", "expert"), None),
            P(("dp", "expert"), None),
            P(("dp", "expert"), None, None),
            P(("dp", "expert"), None),
            P(("dp", "expert"), None),
            P("expert", None, None),
            P("expert", None, None),
            P("expert", None, None),
        ),
        out_specs=(
            P(("dp", "expert"), None),
            P("expert", "dp", None),
            P("expert", "dp", None),
            P("expert", "dp", None),
        ),
        check_vma=False,
    )
```

```python
import functools

import jax
import jax.numpy as jnp
from jax import lax
from jax.experimental import pallas as pl
from jax.experimental.pallas import tpu as pltpu
from jax.sharding import PartitionSpec as P

grad_scale = 0.0625
slot_cap = 48
gate_cuts = (0, 768, 1408)
pieces = 2
early_gates = 9


def mm(a, b, ca, cb):
    return lax.dot_general(a, b, (((ca,), (cb,)), ((), ())), preferred_element_type=jnp.float32)


def dispatch_kernel(
    first,
    meta_ref,
    tok_hbm,
    grad_hbm,
    gate_hbm,
    rows_out,
    routed_out,
    gate_out,
    late_out,
    held,
    rows_st,
    routed_st,
    gate_vm,
    slots,
    late,
    landed,
    slot_of,
    hot_st,
    load_sem,
    send_sem,
    recv_sem,
    gate_send,
    gate_recv,
    late_sem,
    out_sem,
):
    n = slots.shape[0]
    tok = tok_hbm.shape[0]
    cap = slots.shape[1]
    top_k = gate_hbm.shape[0]
    me = lax.axis_index("expert")
    core = me % 2
    x = (me // 2) % 4
    y = me // 8
    sib = me + 1 - 2 * core

    def place(da, db, c):
        dx = da * (1 - c) + db * c
        dy = da * c + db * (1 - c)
        return (((y + dy) % 4) * 4 + (x + dx) % 4) * 2 + c

    loads = [
        pltpu.make_async_copy(tok_hbm, held.at[me, pl.ds(0, tok)], load_sem.at[0]),
        pltpu.make_async_copy(grad_hbm, held.at[me, pl.ds(tok, tok)], load_sem.at[1]),
        pltpu.make_async_copy(gate_hbm, gate_vm, load_sem.at[2]),
    ]
    for load in loads:
        load.start()

    barrier = pltpu.get_barrier_semaphore()

    @pl.loop(1, n)
    def _(d):
        pl.semaphore_signal(
            barrier, inc=1, device_id={"expert": (me + d) % n}, device_id_type=pl.DeviceIdType.MESH
        )

    pl.semaphore_wait(barrier, n - 1)

    sent = []

    piece = held.shape[1] // pieces

    def send(chunk, number, to):
        part = held.at[chunk, pl.ds(number * piece, piece)]
        copy = pltpu.make_async_remote_copy(
            src_ref=part,
            dst_ref=part,
            send_sem=send_sem.at[len(sent)],
            recv_sem=recv_sem.at[chunk, number],
            device_id={"expert": to},
            device_id_type=pl.DeviceIdType.MESH,
        )
        copy.start()
        sent.append(copy)

    def arrive(chunk, number):
        part = held.at[chunk, pl.ds(number * piece, piece)]
        pltpu.make_async_remote_copy(
            src_ref=part,
            dst_ref=part,
            send_sem=send_sem.at[0],
            recv_sem=recv_sem.at[chunk, number],
            device_id={"expert": sib},
            device_id_type=pl.DeviceIdType.MESH,
        ).wait_recv()

    a_up, a_down = place(1, 0, core), place(3, 0, core)
    b_up, b_down = place(0, 1, core), place(0, 3, core)

    for number in range(pieces):
        if number % (pieces // 2) == 0:
            loads[number // (pieces // 2)].wait()
        for to in (a_up, a_down, b_up, b_down, sib):
            send(me, number, to)

    ids = meta_ref[0:top_k, :]
    probs = meta_ref[top_k : 2 * top_k, :]
    peers = lax.broadcasted_iota(jnp.int32, (n, tok), 0).astype(jnp.float32)
    chosen = jnp.zeros((n, tok), jnp.float32)
    for k in range(top_k):
        chosen = jnp.where(peers == ids[k : k + 1, :], 1.0, chosen)
    before = (
        lax.broadcasted_iota(jnp.int32, (tok, tok), 0) < lax.broadcasted_iota(jnp.int32, (tok, tok), 1)
    ).astype(jnp.float32)
    rank = jnp.dot(
        chosen.astype(jnp.bfloat16), before.astype(jnp.bfloat16), preferred_element_type=jnp.float32
    )
    slot_of[...] = jnp.where(chosen > 0.0, rank, -1.0)
    loads[2].wait()

    lane = lax.broadcasted_iota(jnp.int32, (cap, tok), 1)
    lane_f = lane.astype(jnp.float32)
    slot_f = lax.broadcasted_iota(jnp.int32, (cap, tok), 0).astype(jnp.float32)
    gang = hot_st.shape[0] // cap

    @pl.loop(0, n // gang)
    def _(g):
        for i in range(gang):
            e = (me + g * gang + i) % n
            e_f = e.astype(jnp.float32)
            hit = jnp.where(slot_f == slot_of[pl.ds(e, 1), :], 1.0, 0.0)
            prob = jnp.zeros((cap, 1), jnp.float32)
            for k in range(top_k):
                hit_k = jnp.where(ids[k : k + 1, :] == e_f, hit, 0.0)
                hot_st[i * cap : (i + 1) * cap, k * tok : (k + 1) * tok] = hit_k.astype(jnp.bfloat16)
                prob = prob + jnp.sum(hit_k * probs[k : k + 1, :], axis=1, keepdims=True)
            used = jnp.sum(hit, axis=1, keepdims=True)
            index = jnp.sum(hit * lane_f, axis=1, keepdims=True) + 255.0 * (1.0 - used)
            hi = prob.astype(jnp.bfloat16).astype(jnp.float32)
            mid = (prob - hi).astype(jnp.bfloat16).astype(jnp.float32)
            low = prob - hi - mid
            info = jnp.where(
                lane == 0, index, jnp.where(lane == 1, hi, jnp.where(lane == 2, mid, low))
            )
            slots[e, :, first : first + tok] = info.astype(jnp.bfloat16)
        got = jnp.dot(
            hot_st[...], gate_vm[...].reshape(top_k * tok, gate_vm.shape[2]), preferred_element_type=jnp.float32
        ).astype(jnp.bfloat16)
        for i in range(gang):
            e = (me + g * gang + i) % n
            slots[e, :, 0:first] = got[i * cap : (i + 1) * cap, :first]
            late[e] = got[i * cap : (i + 1) * cap, first:]

    late_copy = pltpu.make_async_copy(late, late_out, late_sem)
    late_copy.start()
    landed[me] = slots[me]
    events = [(3, 0), (1, 0), (0, 3), (0, 1), (2, 0), (0, 2)]
    events += [(da, db) for da in (3, 1, 2) for db in (3, 1, 2)]
    to_send = [(0, 0, 1)] + [(4 - da, 4 - db, flip) for da, db in events for flip in range(2)]

    def gate_sends(count):
        for da, db, flip in to_send[:count]:
            e = place(da, db, core) + flip * (1 - 2 * core)
            pltpu.make_async_remote_copy(
                src_ref=slots.at[e],
                dst_ref=landed.at[me],
                send_sem=gate_send.at[e],
                recv_sem=gate_recv.at[me],
                device_id={"expert": e},
                device_id_type=pl.DeviceIdType.MESH,
            ).start()
        del to_send[:count]

    gate_sends(early_gates)

    def gate_copy(peer):
        return pltpu.make_async_remote_copy(
            src_ref=slots.at[peer],
            dst_ref=landed.at[peer],
            send_sem=gate_send.at[peer],
            recv_sem=gate_recv.at[peer],
            device_id={"expert": peer},
            device_id_type=pl.DeviceIdType.MESH,
        )

    outs = []

    def pick(chunk):
        info = landed[chunk, :, first : first + tok].astype(jnp.float32)
        hot = jnp.where(lane_f == info[:, 0:1], 1.0, 0.0).astype(jnp.bfloat16)
        prob = info[:, 1:2] + info[:, 2:3] + info[:, 3:4]
        rows_st[chunk] = jnp.dot(
            hot, held[chunk, 0:tok, :], preferred_element_type=jnp.float32
        ).astype(jnp.bfloat16)
        routed_st[chunk] = (
            prob * jnp.dot(hot, held[chunk, tok : 2 * tok, :], preferred_element_type=jnp.float32)
        ).astype(jnp.bfloat16)
        number = len(outs)
        copies = (
            pltpu.make_async_copy(rows_st.at[chunk], rows_out.at[chunk], out_sem.at[number]),
            pltpu.make_async_copy(routed_st.at[chunk], routed_out.at[chunk], out_sem.at[n + number]),
            pltpu.make_async_copy(
                landed.at[chunk, :, pl.ds(0, first)], gate_out.at[chunk], out_sem.at[2 * n + number]
            ),
        )
        for copy in copies:
            copy.start()
        outs.append(copies)

    def from_sibling(da, db):
        chunk = place(da, db, 1 - core)
        gate_copy(chunk).wait_recv()
        for number in range(pieces):
            arrive(chunk, number)
        pick(chunk)

    pick(me)
    behind = [(0, 0)]
    for da, db in events:
        chunk = place(da, db, core)
        low, high = range(pieces // 2), range(pieces // 2, pieces)
        side = da if db == 0 else db
        for number in (*high, *low) if side == 1 else (*low, *high):
            arrive(chunk, number)
            up, down = (a_up, a_down) if db == 0 else (b_up, b_down)
            if side == 3 and number in low:
                send(chunk, number, up)
            if side == 1 and number in high:
                send(chunk, number, down)
            if db == 0:
                send(chunk, number, b_up)
                send(chunk, number, b_down)
            send(chunk, number, sib)
        gate_sends(2)
        gate_copy(chunk).wait_recv()
        pick(chunk)
        from_sibling(*behind.pop())
        behind.append((da, db))
    from_sibling(*behind.pop())

    for copy in sent:
        copy.wait_send()

    @pl.loop(1, n)
    def _(d):
        gate_copy((me + d) % n).wait_send()

    late_copy.wait()
    for copies in outs:
        for copy in copies:
            copy.wait()


def dispatch(meta, tokens, out_grad, gate_by_k):
    n = lax.axis_size("expert")
    tok, width = tokens.shape
    top_k, _, hidden = gate_by_k.shape
    first = gate_cuts[1]
    bf16 = jnp.bfloat16
    anywhere = pl.BlockSpec(memory_space=pl.ANY)
    return pl.pallas_call(
        functools.partial(dispatch_kernel, first),
        out_shape=(
            jax.ShapeDtypeStruct((n, slot_cap, width), bf16),
            jax.ShapeDtypeStruct((n, slot_cap, width), bf16),
            jax.ShapeDtypeStruct((n, slot_cap, first), bf16),
            jax.ShapeDtypeStruct((n, slot_cap, hidden - first), bf16),
        ),
        in_specs=[pl.BlockSpec(memory_space=pltpu.VMEM), anywhere, anywhere, anywhere],
        out_specs=(anywhere,) * 4,
        scratch_shapes=[
            pltpu.VMEM((n, 2 * tok, width), bf16),
            pltpu.VMEM((n, slot_cap, width), bf16),
            pltpu.VMEM((n, slot_cap, width), bf16),
            pltpu.VMEM((top_k, tok, hidden), bf16),
            pltpu.VMEM((n, slot_cap, first + tok), bf16),
            pltpu.VMEM((n, slot_cap, hidden - first), bf16),
            pltpu.VMEM((n, slot_cap, first + tok), bf16),
            pltpu.VMEM((n, tok), jnp.float32),
            pltpu.VMEM((4 * slot_cap, top_k * tok), bf16),
            pltpu.SemaphoreType.DMA((3,)),
            pltpu.SemaphoreType.DMA((31 * pieces,)),
            pltpu.SemaphoreType.DMA((n, pieces)),
            pltpu.SemaphoreType.DMA((n,)),
            pltpu.SemaphoreType.DMA((n,)),
            pltpu.SemaphoreType.DMA,
            pltpu.SemaphoreType.DMA((3 * n,)),
        ],
        compiler_params=pltpu.CompilerParams(
            collective_id=0, has_side_effects=True, vmem_limit_bytes=62 << 20
        ),
        cost_estimate=pl.CostEstimate(
            flops=8 * n * slot_cap * tok * width, bytes_accessed=100 << 20, transcendentals=0
        ),
    )(meta, tokens, out_grad, gate_by_k)


def reduce_kernel(
    cuts,
    *refs,
):
    sources, refs = refs[:8], refs[8:]
    loaded, refs = refs[6 : 6 + 8], refs[:6] + refs[6 + 8 :]
    reduce_body(cuts, sources, loaded, *refs)


def reduce_body(
    cuts,
    sources,
    loaded,
    gate_mat,
    up_mat,
    gate_out,
    up_out,
    down_out,
    returned,
    hidden_ref,
    back,
    mats,
    wide,
    tall,
    wide_first,
    tall_first,
    wide_send,
    wide_recv,
    tall_send,
    tall_recv,
    mat_sem,
    back_send,
    back_recv,
    own_sem,
    load_sem,
):
    gate_1st, up_1st, gate_ref, up_ref, rows_ref, hidden_1st, hidden_2nd, routed_ref = loaded
    loads = [
        pltpu.make_async_copy(source, loaded[i], load_sem.at[i]) for i, source in enumerate(sources)
    ]
    n = hidden_ref.shape[0]
    n_peers, cap = back.shape[:2]
    here = lax.axis_index("expert")
    first = cuts[1]
    me = lax.axis_index("dp")
    quarter = gate_out.shape[0]
    half = tall_first.shape[2]
    ahead, behind = (me + 1) % n, (me + n - 1) % n

    tile = mats.shape[2]
    n_tiles = gate_mat.shape[0] // tile

    def mat_loads(t):
        return [
            pltpu.make_async_copy(
                mat.at[pl.ds(t * tile, tile)], mats.at[t % 2, i], mat_sem.at[t % 2, i]
            )
            for i, mat in enumerate((gate_mat, up_mat))
        ]

    for i in (2, 3, 4, 0, 1):
        loads[i].start()
    for load in mat_loads(0):
        load.start()
    for load in loads[5:]:
        load.start()
    for load in mat_loads(1):
        load.start()

    barrier = pltpu.get_barrier_semaphore()
    for to in (ahead, behind):
        pl.semaphore_signal(
            barrier, inc=1, device_id={"dp": to}, device_id_type=pl.DeviceIdType.MESH
        )

    @pl.loop(1, n_peers)
    def _(d):
        pl.semaphore_signal(
            barrier,
            inc=1,
            device_id={"expert": (here + d) % n_peers},
            device_id_type=pl.DeviceIdType.MESH,
        )

    pl.semaphore_wait(barrier, n_peers + 1)

    def copy_of(which, way, hop):
        first, landed, send_sem, recv_sem = (
            (wide_first, wide, wide_send, wide_recv) if which == 0 else (tall_first, tall, tall_send, tall_recv)
        )
        return pltpu.make_async_remote_copy(
            src_ref=first.at[way] if hop == 0 else landed.at[way, hop - 1],
            dst_ref=landed.at[way, hop],
            send_sem=send_sem.at[way, hop],
            recv_sem=recv_sem.at[way, hop],
            device_id={"dp": ahead if way == 0 else behind},
            device_id_type=pl.DeviceIdType.MESH,
        )

    def term(which, way, share):
        if which == 0:
            columns = pl.ds(pl.multiple_of(share * quarter, quarter), quarter)
            got = mm(rows_ref[:, columns], (gate_ref if way == 0 else up_ref)[...], 0, 0)
        else:
            got = mm(hidden_ref[share], routed_ref[:, way * half : (way + 1) * half], 0, 0)
        return grad_scale * got

    def step(hop, which):
        for way in range(2):
            share = (me + n - 1 - hop) % n if way == 0 else (me + 1 + hop) % n
            part = term(which, way, share)
            if hop == 0:
                start = wide_first if which == 0 else tall_first
                start[way] = part.astype(jnp.bfloat16)
            else:
                landed = wide if which == 0 else tall
                copy_of(which, way, hop - 1).wait_recv()
                part = (part + landed[way, hop - 1].astype(jnp.float32)).astype(jnp.bfloat16)
                if hop < n - 1:
                    landed[way, hop - 1] = part
                elif which == 0:
                    (gate_out if way == 0 else up_out)[...] = part
                else:
                    down_out[:, way * half : (way + 1) * half] = part
            if hop < n - 1:
                copy_of(which, way, hop).start()

    def split_hidden():
        tall_rows = hidden_ref.shape[2]
        row_block = 256

        @pl.loop(0, hidden_ref.shape[1] // row_block)
        def _(r):
            rows = pl.ds(pl.multiple_of(r * row_block, row_block), row_block)
            for q in range(n):
                for source, a, b in ((hidden_1st, 0, first), (hidden_2nd, first, cuts[2])):
                    low, high = max(a, q * tall_rows), min(b, (q + 1) * tall_rows)
                    if low < high:
                        hidden_ref[q, rows, low - q * tall_rows : high - q * tall_rows] = source[
                            rows, low - a : high - a
                        ]

    gang = 8
    n_gangs = n_peers // gang

    def back_copy(part, peer, at):
        columns = pl.ds(part * tile, tile)
        return pltpu.make_async_remote_copy(
            src_ref=back.at[peer, :, columns],
            dst_ref=returned.at[at, :, columns],
            send_sem=back_send.at[part, peer],
            recv_sem=back_recv.at[part, at],
            device_id={"expert": peer},
            device_id_type=pl.DeviceIdType.MESH,
        )

    def input_tile(t):
        for load in mat_loads(t):
            load.wait()

        @pl.loop(0, n_gangs)
        def _(m):
            rows = pl.ds(pl.multiple_of(m * gang * cap, gang * cap), gang * cap)
            total = mm(gate_1st[rows, :], mats[t % 2, 0, :, :first], 1, 1)
            total = total + mm(gate_ref[rows, :], mats[t % 2, 0, :, first:], 1, 1)
            total = total + mm(up_1st[rows, :], mats[t % 2, 1, :, :first], 1, 1)
            total = total + mm(up_ref[rows, :], mats[t % 2, 1, :, first:], 1, 1)
            back[pl.ds(m * gang, gang), :, t * tile : (t + 1) * tile] = total.astype(
                jnp.bfloat16
            ).reshape(gang, cap, tile)

        if t + 2 < n_tiles:
            for load in mat_loads(t + 2):
                load.start()
        @pl.loop(1, n_peers)
        def _(d):
            back_copy(t, (here + d) % n_peers, here).start()

    for i in (2, 3, 4):
        loads[i].wait()
    step(0, 0)
    for i in (0, 1):
        loads[i].wait()
    input_tile(0)
    for load in loads[5:]:
        load.wait()
    split_hidden()
    step(0, 1)
    input_tile(1)
    step(1, 0)
    input_tile(2)
    input_tile(3)

    own = pltpu.make_async_copy(back.at[here], returned.at[here], own_sem)
    own.start()

    step(1, 1)
    for hop in range(2, n):
        for which in range(2):
            step(hop, which)

    for hop in range(n - 1):
        for which in range(2):
            for way in range(2):
                copy_of(which, way, hop).wait_send()
    own.wait()
    for part in range(n_tiles):

        @pl.loop(1, n_peers)
        def _(d):
            peer = (here + d) % n_peers
            back_copy(part, peer, peer).wait_recv()
            back_copy(part, peer, peer).wait_send()


def reduce_late(rows_in, routed, grads, hidden, gate_mat, up_mat):
    n = lax.axis_size("dp")
    n_peers = lax.axis_size("expert")
    slots, width = rows_in.shape
    cols = gate_cuts[2] - gate_cuts[1]
    tall_rows = gate_cuts[2] // n
    quarter, half, tile = width // n, width // 2, width // 4
    bf16 = jnp.bfloat16
    vmem = pl.BlockSpec(memory_space=pltpu.VMEM)
    anywhere = pl.BlockSpec(memory_space=pl.ANY)
    sources = (*grads, rows_in, *hidden, routed)
    return pl.pallas_call(
        functools.partial(reduce_kernel, gate_cuts),
        out_shape=(
            jax.ShapeDtypeStruct((quarter, cols), bf16),
            jax.ShapeDtypeStruct((quarter, cols), bf16),
            jax.ShapeDtypeStruct((tall_rows, width), bf16),
            jax.ShapeDtypeStruct((n_peers, slot_cap, width), bf16),
        ),
        in_specs=[anywhere] * 10,
        out_specs=(vmem, vmem, vmem, anywhere),
        scratch_shapes=[pltpu.VMEM(source.shape, bf16) for source in sources]
        + [
            pltpu.VMEM((n, slots, tall_rows), bf16),
            pltpu.VMEM((n_peers, slot_cap, width), bf16),
            pltpu.VMEM((2, 2, tile, gate_cuts[2]), bf16),
            pltpu.VMEM((2, n - 1, quarter, cols), bf16),
            pltpu.VMEM((2, n - 1, tall_rows, half), bf16),
            pltpu.VMEM((2, quarter, cols), bf16),
            pltpu.VMEM((2, tall_rows, half), bf16),
            pltpu.SemaphoreType.DMA((2, n - 1)),
            pltpu.SemaphoreType.DMA((2, n - 1)),
            pltpu.SemaphoreType.DMA((2, n - 1)),
            pltpu.SemaphoreType.DMA((2, n - 1)),
            pltpu.SemaphoreType.DMA((2, 2)),
            pltpu.SemaphoreType.DMA((4, n_peers)),
            pltpu.SemaphoreType.DMA((4, n_peers)),
            pltpu.SemaphoreType.DMA,
            pltpu.SemaphoreType.DMA((8,)),
        ],
        compiler_params=pltpu.CompilerParams(
            collective_id=1, has_side_effects=True, vmem_limit_bytes=63 << 20
        ),
        cost_estimate=pl.CostEstimate(
            flops=2 * slots * width * (4 * cols + 3 * n * tall_rows),
            bytes_accessed=300 << 20,
            transcendentals=0,
        ),
    )(*sources, gate_mat, up_mat)


def local(tokens, out_grad, gate_saved, probs, expert_ids, w_gate, w_up, w_down):
    n_peers = lax.axis_size("expert")
    tok_rows, model_width = tokens.shape
    top_k = expert_ids.shape[1]
    n_slots = n_peers * slot_cap
    gate_mat, up_mat, down_mat = w_gate[0], w_up[0], w_down[0]

    ids_t = expert_ids.T
    meta = jnp.concatenate(
        [ids_t.astype(jnp.float32), probs.T, jnp.zeros((16 - 2 * top_k, tok_rows), jnp.float32)], axis=0
    )
    rows_in, routed, gate_first, gate_late = dispatch(
        meta, tokens, out_grad, jnp.transpose(gate_saved, (1, 0, 2))
    )
    rows_in = rows_in.reshape(n_slots, model_width)
    routed = routed.reshape(n_slots, model_width)
    gate_late = lax.all_to_all(gate_late, "expert", split_axis=0, concat_axis=0, tiled=True)
    recv_gate = [g.reshape(n_slots, g.shape[2]) for g in (gate_first, gate_late)]

    experts = lax.broadcasted_iota(jnp.int32, (n_peers, 1, 1), 0)
    chosen = jnp.any(ids_t[None] == experts, axis=1)
    before = (
        lax.broadcasted_iota(jnp.int32, (tok_rows, tok_rows), 0)
        < lax.broadcasted_iota(jnp.int32, (tok_rows, tok_rows), 1)
    ).astype(jnp.bfloat16)
    rank = mm(chosen.astype(jnp.bfloat16), before, 1, 0).astype(jnp.int32)
    slots = lax.broadcasted_iota(jnp.int32, (1, slot_cap, 1), 1)
    send_hot = (rank[:, None, :] == slots) & chosen[:, None, :]

    hidden, gate_grads, up_grads, first_share = [], [], [], None
    for j, (a, b) in enumerate(zip(gate_cuts, gate_cuts[1:])):
        hidden_grad = mm(routed, down_mat[a:b, :], 1, 1)
        up_act = mm(rows_in, up_mat[:, a:b], 1, 0)
        gate_val = recv_gate[j].astype(jnp.float32)
        gate_sig = jax.nn.sigmoid(gate_val)
        gate_act = gate_val * gate_sig
        hidden.append((gate_act * up_act).astype(jnp.bfloat16))
        up_grad = (hidden_grad * gate_act).astype(jnp.bfloat16)
        gate_grad = (hidden_grad * up_act * gate_sig * (1.0 + gate_val * (1.0 - gate_sig))).astype(
            jnp.bfloat16
        )
        gate_grads.append(gate_grad)
        up_grads.append(up_grad)
        if j == 0:
            both = jnp.concatenate([gate_grad, up_grad], axis=1)
            term = (grad_scale * mm(rows_in, both, 0, 0)).astype(jnp.bfloat16)
            first_share = lax.psum_scatter(term, "dp", scatter_dimension=0, tiled=True)

    grads = (gate_grads[0], up_grads[0], gate_grads[1], up_grads[1])
    late_gate, late_up, grad_down, returned = reduce_late(
        rows_in, routed, grads, hidden, gate_mat, up_mat
    )
    input_grad = mm(
        send_hot.reshape(n_slots, tok_rows).astype(jnp.bfloat16),
        returned.reshape(n_slots, model_width),
        0,
        0,
    ).astype(jnp.bfloat16)

    first = gate_cuts[1]
    grad_gate = jnp.concatenate([first_share[:, :first], late_gate], axis=1)
    grad_up = jnp.concatenate([first_share[:, first:], late_up], axis=1)
    return (input_grad, grad_gate[None], grad_up[None], grad_down[None])


def solution(mesh):
    return jax.shard_map(
        local,
        mesh=mesh,
        in_specs=(
            P(("dp", "expert"), None),
            P(("dp", "expert"), None),
            P(("dp", "expert"), None, None),
            P(("dp", "expert"), None),
            P(("dp", "expert"), None),
            P("expert", None, None),
            P("expert", None, None),
            P("expert", None, None),
        ),
        out_specs=(
            P(("dp", "expert"), None),
            P("expert", "dp", None),
            P("expert", "dp", None),
            P("expert", "dp", None),
        ),
        check_vma=False,
    )
```
